256 devices in a mesh: sx: 16 (over z, core), sy: 16 (over x, y).
Axes of the slice: x: 4, y: 4, z: 8, core: 2. Of those that a mesh axis runs over, the one named last changes fastest.
Arguments:
- source: float32 [3, 64, 128, 128], P(None, 'sx', 'sy'), may hold values from -12 to 12
- initial_guess: float32 [3, 64, 128, 128], P(None, 'sx', 'sy'), may hold values from -6 to 6
- coupling: float32 [3, 3, 3, 64, 128, 128], P(None, None, None, 'sx', 'sy'), may hold values from -1.25 to 0.25
- diagonal_block: float32 [3, 3, 64, 128, 128], P(None, None, 'sx', 'sy'), may hold values from -0.15 to 15, as said below
- prolongator: float32 [3, 3, 64, 128, 128], P(None, None, 'sx', 'sy'), may hold values from -4 to 4
- aggregate: int32 [64, 128, 128], P('sx', 'sy'), may hold values from 0 to 127, as said below
Outputs:
- solution: float32 [3, 64, 128, 128], P(None, 'sx', 'sy')
- coarse_correction: float32 [3, 16, 16, 128], P(None, 'sx', 'sy')
The draws below stay inside these ranges and needn't reach their ends.
Inputs may be any that keep to these rules, and one draw needn't show every extreme that they name: `diagonal_block`: each node's 3x3 block is symmetric. `aggregate`: ids are local to the subdomain of 4 x 8 x 128 nodes held by one device; every id occurs in every subdomain.
All inputs are finite; a program needn't handle non-finite values.
Results may differ from the reference program's by a relative error of at most 0.0003.
Values sent between devices are 32-bit elements; how exact they have to be, the bound alone decides.
No kernel may reach another device: no remote copies, remote signals or barrier semaphores. Data moves between devices by JAX's collectives and lax.ppermute only.
A program may use at most 128 MiB of HBM per device.

```python
import jax
import jax.numpy as jnp
from jax import lax

BX = 4
BY = 8
BZ = 128
AGG = 32
NU = 2
KC = 4
NA = 128
NX = 64
NY = 128
N_SX = 16
N_SY = 16


def draw_source(key, part):
    across_x = jnp.arange(NX, dtype=jnp.float32) / (NX - 1)
    across_y = jnp.arange(NY, dtype=jnp.float32) / (NY - 1)
    scaling = 1.0 + across_x[:, None, None] + across_y[None, :, None]
    noise = jax.random.truncated_normal(key, -4.0, 4.0, (3, NX, NY, BZ), jnp.float32)
    return noise * scaling[None]


def draw_coupling(key, part):
    first, second = jax.random.split(key)
    strength = jnp.exp(jax.random.uniform(first, (3, NX, NY, BZ), jnp.float32, -0.6931472, 0.0))
    noise = 0.25 * jax.random.uniform(second, (3, 3, 3, NX, NY, BZ), jnp.float32, -1.0, 1.0)
    identity = jnp.eye(3, dtype=jnp.float32)[None, :, :, None, None, None]
    return -(identity * strength[:, None, None] + noise)


def draw_diagonal_block(key, part):
    first, second = jax.random.split(key)
    level = 11.0 + 4.0 * jax.random.uniform(first, (NX, NY, BZ), jnp.float32)
    offdiag = 0.15 * jax.random.uniform(second, (3, NX, NY, BZ), jnp.float32, -1.0, 1.0)
    entries = [[level, offdiag[0], offdiag[1]], [offdiag[0], level, offdiag[2]], [offdiag[1], offdiag[2], level]]
    return jnp.stack([jnp.stack(row_items) for row_items in entries])


def draw_aggregate(key, part):
    first, second = jax.random.split(key)
    local_x = jnp.arange(NX, dtype=jnp.int32) % BX
    local_y = jnp.arange(NY, dtype=jnp.int32) % BY
    local_z = jnp.arange(BZ, dtype=jnp.int32)
    linear = (local_x[:, None, None] * BY + local_y[None, :, None]) * BZ + local_z[None, None, :]
    base = linear // AGG
    leader = linear % AGG == 0
    picked = jax.random.randint(first, (NX, NY, BZ), 0, 4) == 0
    other = jax.random.randint(second, (NX, NY, BZ), 0, NA)
    return jnp.where(picked & jnp.logical_not(leader), other, base).astype(jnp.int32)


def block_levels(rng, shape, cuts, least, largest):
    loudness = 1.0
    for dim, parts in cuts:
        steps = jax.random.uniform(jax.random.fold_in(jax.random.fold_in(rng, 6), dim), (parts,), jnp.float32, least / len(cuts), largest / len(cuts))
        loudness = loudness * jnp.repeat(jnp.exp(steps), shape[dim] // parts).reshape((-1,) + (1,) * (len(shape) - 1 - dim))
    return loudness


def scatter_about(key, dims, spread, reach, cuts=(), held_as=jnp.bfloat16):
    array = spread * jax.random.normal(key, dims, jnp.float32)
    if cuts:
        array = array * block_levels(key, dims, cuts, -0.22, 0.18)
    return jnp.clip(array, -reach, reach).astype(held_as)


def setup_inputs(seed: int = 0) -> dict:
    splits = jax.random.split(jax.random.key(seed), 7)
    source = draw_source(jax.random.fold_in(splits[6], 71), 0)
    initial_guess = scatter_about(splits[1], (3, NX, NY, BZ), 1.0, 6.0, ((1, 16), (2, 16)), jnp.float32)
    coupling = draw_coupling(jax.random.fold_in(splits[6], 71), 0)
    diagonal_block = draw_diagonal_block(jax.random.fold_in(splits[6], 71), 0)
    prolongator = scatter_about(splits[4], (3, 3, NX, NY, BZ), 1.0, 4.0, ((2, 16), (3, 16)), jnp.float32)
    aggregate = draw_aggregate(jax.random.fold_in(splits[6], 71), 0)
    return dict(source=source, initial_guess=initial_guess, coupling=coupling, diagonal_block=diagonal_block, prolongator=prolongator, aggregate=aggregate)


damping = 0.8
highest = lax.Precision.HIGHEST


def invert_blocks(matrix):
    adjugate = [[matrix[(j + 1) % 3, (i + 1) % 3] * matrix[(j + 2) % 3, (i + 2) % 3] - matrix[(j + 1) % 3, (i + 2) % 3] * matrix[(j + 2) % 3, (i + 1) % 3] for j in range(3)] for i in range(3)]
    determinant = matrix[0, 0] * adjugate[0][0] + matrix[0, 1] * adjugate[1][0] + matrix[0, 2] * adjugate[2][0]
    return jnp.stack([jnp.stack([adjugate[i][j] / determinant for j in range(3)]) for i in range(3)])


def apply_block(matrix, vector):
    return jnp.stack([matrix[i, 0] * vector[0] + matrix[i, 1] * vector[1] + matrix[i, 2] * vector[2] for i in range(3)])


def apply_transposed(matrix, vector):
    return jnp.stack([matrix[0, i] * vector[0] + matrix[1, i] * vector[1] + matrix[2, i] * vector[2] for i in range(3)])


def triple(left, middle, right):
    inner = [[middle[i, 0] * right[0, l] + middle[i, 1] * right[1, l] + middle[i, 2] * right[2, l] for l in range(3)] for i in range(3)]
    return jnp.stack([jnp.stack([left[0, k] * inner[0][l] + left[1, k] * inner[1][l] + left[2, k] * inner[2][l] for l in range(3)]) for k in range(3)])


def scatter_blocks(portions):
    values = jnp.concatenate([portion[0].reshape(9, -1) for portion in portions], axis=1)
    targets = jnp.concatenate([(portion[1].reshape(-1) * NA + portion[2].reshape(-1)).astype(jnp.int32) for portion in portions])
    summed = jnp.zeros((9, NA * NA), jnp.float32).at[:, targets].add(values)
    return summed.reshape(3, 3, NA, NA).transpose(0, 2, 1, 3).reshape(3 * NA, 3 * NA)


def galerkin_blocks(diagonal_block, coupling, prolong_ext, groups_ext):
    prolong = prolong_ext[:, :, 1:-1, 1:-1]
    groups = groups_ext[1:-1, 1:-1]
    self_term = triple(prolong, diagonal_block, prolong)
    x_term = triple(prolong[:, :, :-1], coupling[0][:, :, :-1], prolong[:, :, 1:])
    y_term = triple(prolong[:, :, :, :-1], coupling[1][:, :, :, :-1], prolong[:, :, :, 1:])
    z_term = triple(prolong[..., :-1], coupling[2][..., :-1], prolong[..., 1:])
    half = scatter_blocks([(0.5 * self_term, groups, groups), (x_term, groups[:-1], groups[1:]), (y_term, groups[:, :-1], groups[:, 1:]), (z_term, groups[..., :-1], groups[..., 1:])])
    local_block = half + half.T
    face_x = triple(prolong[:, :, -1], coupling[0][:, :, -1], prolong_ext[:, :, -1, 1:-1])
    face_y = triple(prolong[:, :, :, -1], coupling[1][:, :, :, -1], prolong_ext[:, :, 1:-1, -1])
    plus_x = scatter_blocks([(face_x, groups[-1], groups_ext[-1, 1:-1])])
    plus_y = scatter_blocks([(face_y, groups[:, -1], groups_ext[1:-1, -1])])
    return local_block, plus_x, plus_y


def apply_operator(field, diagonal_block, coupling):
    padded = jnp.pad(field, ((0, 0), (1, 1), (1, 1), (1, 1)))
    couple_pad = jnp.pad(coupling, ((0, 0), (0, 0), (0, 0), (1, 1), (1, 1), (1, 1)))
    result = apply_block(diagonal_block, field)
    result = result + apply_block(coupling[0], padded[:, 2:, 1:-1, 1:-1])
    result = result + apply_block(coupling[1], padded[:, 1:-1, 2:, 1:-1])
    result = result + apply_block(coupling[2], padded[:, 1:-1, 1:-1, 2:])
    result = result + apply_transposed(couple_pad[0, :, :, :-2, 1:-1, 1:-1], padded[:, :-2, 1:-1, 1:-1])
    result = result + apply_transposed(couple_pad[1, :, :, 1:-1, :-2, 1:-1], padded[:, 1:-1, :-2, 1:-1])
    result = result + apply_transposed(couple_pad[2, :, :, 1:-1, 1:-1, :-2], padded[:, 1:-1, 1:-1, :-2])
    return result


def subdomain_blocks(index, diagonal_block, coupling, prolong_pad, group_pad):
    start_x = (index // N_SY).astype(jnp.int32) * BX
    start_y = (index % N_SY).astype(jnp.int32) * BY
    anchor = jnp.zeros((), jnp.int32)
    own_diag = lax.dynamic_slice(diagonal_block, (anchor, anchor, start_x, start_y, anchor), (3, 3, BX, BY, BZ))
    own_couple = lax.dynamic_slice(coupling, (anchor, anchor, anchor, start_x, start_y, anchor), (3, 3, 3, BX, BY, BZ))
    prolong_ext = lax.dynamic_slice(prolong_pad, (anchor, anchor, start_x, start_y, anchor), (3, 3, BX + 2, BY + 2, BZ))
    groups_ext = lax.dynamic_slice(group_pad, (start_x, start_y, anchor), (BX + 2, BY + 2, BZ))
    return galerkin_blocks(own_diag, own_couple, prolong_ext, groups_ext)


def coarse_apply(vector, local_all, plus_x_all, plus_y_all):
    result = jnp.einsum('abij,abj->abi', local_all, vector, precision=highest)
    after_x = jnp.pad(vector[1:], ((0, 1), (0, 0), (0, 0)))
    result = result + jnp.einsum('abij,abj->abi', plus_x_all, after_x, precision=highest)
    back_x = jnp.einsum('abji,abj->abi', plus_x_all, vector, precision=highest)
    result = result + jnp.pad(back_x[:-1], ((1, 0), (0, 0), (0, 0)))
    after_y = jnp.pad(vector[:, 1:], ((0, 0), (0, 1), (0, 0)))
    result = result + jnp.einsum('abij,abj->abi', plus_y_all, after_y, precision=highest)
    back_y = jnp.einsum('abji,abj->abi', plus_y_all, vector, precision=highest)
    result = result + jnp.pad(back_y[:, :-1], ((0, 0), (1, 0), (0, 0)))
    return result


def reference(source, initial_guess, coupling, diagonal_block, prolongator, aggregate):
    inverse_diag = invert_blocks(diagonal_block)

    def sweeps(field):
        for sweep_number in range(NU):
            field = field + damping * apply_block(inverse_diag, source - apply_operator(field, diagonal_block, coupling))
        return field

    smoothed = sweeps(initial_guess)
    residual = source - apply_operator(smoothed, diagonal_block, coupling)
    projected = apply_transposed(prolongator, residual)
    devices = N_SX * N_SY
    owner_x = jnp.arange(NX, dtype=jnp.int32) // BX
    owner_y = jnp.arange(NY, dtype=jnp.int32) // BY
    owner = owner_x[:, None, None] * N_SY + owner_y[None, :, None] + jnp.zeros((NX, NY, BZ), jnp.int32)
    targets = (owner * NA + aggregate).reshape(-1).astype(jnp.int32)
    coarse_rhs = jnp.zeros((3, devices * NA), jnp.float32).at[:, targets].add(projected.reshape(3, -1))
    vector_rhs = coarse_rhs.reshape(3, N_SX, N_SY, NA).transpose(1, 2, 0, 3).reshape(N_SX, N_SY, 3 * NA)
    prolong_pad = jnp.pad(prolongator, ((0, 0), (0, 0), (1, 1), (1, 1), (0, 0)))
    group_pad = jnp.pad(aggregate, ((1, 1), (1, 1), (0, 0)))
    local_all, plus_x_all, plus_y_all = lax.map(lambda index: subdomain_blocks(index, diagonal_block, coupling, prolong_pad, group_pad), jnp.arange(devices, dtype=jnp.int32))
    local_all = local_all.reshape(N_SX, N_SY, 3 * NA, 3 * NA)
    plus_x_all = plus_x_all.reshape(N_SX, N_SY, 3 * NA, 3 * NA)
    plus_y_all = plus_y_all.reshape(N_SX, N_SY, 3 * NA, 3 * NA)
    correction = jnp.zeros_like(vector_rhs)
    remaining = vector_rhs
    direction = vector_rhs
    norm_now = jnp.sum(remaining * remaining)
    for iteration in range(KC):
        image = coarse_apply(direction, local_all, plus_x_all, plus_y_all)
        alpha = norm_now / jnp.sum(direction * image)
        correction = correction + alpha * direction
        remaining = remaining - alpha * image
        norm_next = jnp.sum(remaining * remaining)
        direction = remaining + (norm_next / norm_now) * direction
        norm_now = norm_next
    coarse_out = correction.reshape(N_SX, N_SY, 3, NA).transpose(2, 0, 1, 3)
    gathered = coarse_out.reshape(3, devices * NA)[:, targets].reshape(3, NX, NY, BZ)
    corrected = smoothed + apply_block(prolongator, gathered)
    return sweeps(corrected), coarse_out
```

```python
import functools

import jax
import jax.numpy as jnp
from jax import lax
from jax.experimental import pallas as pl
from jax.experimental.pallas import tpu as pltpu
from jax.sharding import PartitionSpec as P

NU = 2
KC = 4
NA = 128
LANES = 128

damping = 0.8
R3 = range(3)
VMEM = pltpu.VMEM
f32 = jnp.float32
bf16 = jnp.bfloat16

PAIRS = [(i, i + lag) for lag in range(KC + 1) for i in range(KC) if i + lag <= KC]
LAG_START = [min(p for p, (i, j) in enumerate(PAIRS) if j - i == lag) for lag in range(KC + 1)]
LAG_COUNT = [sum(1 for i, j in PAIRS if j - i == lag) for lag in range(KC + 1)]


def pair_exchange(x, axis, odd):
    n = lax.axis_size(axis)
    if odd:
        pairs = [(k, (k + 1) % n) for k in range(1, n, 2)] + [((k + 1) % n, k) for k in range(1, n, 2)]
    else:
        pairs = [(k, k ^ 1) for k in range(n)]
    return lax.ppermute(x, axis, pairs)


def exchange(sends):
    xa, xb, ya, yb = sends
    return (
        pair_exchange(xa, "sx", False),
        pair_exchange(xb, "sx", True),
        pair_exchange(ya, "sy", False),
        pair_exchange(yb, "sy", True),
    )


def iota(shape, dim):
    return lax.broadcasted_iota(jnp.int32, shape, dim)


def sides(axis):
    index = lax.axis_index(axis)
    return index % 2 == 0, index == 0, index == lax.axis_size(axis) - 1


def load_field(ref):
    return [[ref[c, x] for x in range(ref.shape[1])] for c in R3]


def store_field(ref, field):
    for c in R3:
        for x in range(ref.shape[1]):
            ref[c, x] = field[c][x]


def times(block, vector):
    return [block(i, 0) * vector[0] + block(i, 1) * vector[1] + block(i, 2) * vector[2] for i in R3]


def transposed_times(block, vector):
    return [block(0, i) * vector[0] + block(1, i) * vector[1] + block(2, i) * vector[2] for i in R3]


def send_faces(field, coupling, sends):
    xa, xb, ya, yb = sends
    nx = len(field[0])
    ny = field[0][0].shape[0]
    even_x, _, _ = sides("sx")
    even_y, _, _ = sides("sy")
    top = transposed_times(lambda i, j: coupling[0, i, j, nx - 1], [field[j][nx - 1] for j in R3])
    for i in R3:
        bottom = field[i][0]
        xa[i] = jnp.where(even_x, top[i], bottom)
        xb[i] = jnp.where(even_x, bottom, top[i])
    for x in range(nx):
        top = transposed_times(
            lambda i, j: coupling[1, i, j, x, ny - 1 : ny], [field[j][x][ny - 1 : ny] for j in R3]
        )
        for i in R3:
            bottom = field[i][x][0:1]
            row = i * nx + x
            ya[row : row + 1] = jnp.where(even_y, top[i], bottom)
            yb[row : row + 1] = jnp.where(even_y, bottom, top[i])


def halos(received, nx):
    xa, xb, ya, yb = received
    even_x, first_x, last_x = sides("sx")
    even_y, first_y, last_y = sides("sy")
    up_x = [jnp.where(last_x, 0.0, jnp.where(even_x, xa[i], xb[i])) for i in R3]
    low_x = [jnp.where(first_x, 0.0, jnp.where(even_x, xb[i], xa[i])) for i in R3]
    up_y = jnp.where(last_y, 0.0, jnp.where(even_y, ya, yb))
    low_y = jnp.where(first_y, 0.0, jnp.where(even_y, yb, ya))
    up_y = [[up_y[i * nx + x : i * nx + x + 1] for x in range(nx)] for i in R3]
    low_y = [[low_y[i * nx + x : i * nx + x + 1] for x in range(nx)] for i in R3]
    return up_x, low_x, up_y, low_y


def read_halos(refs):
    xa, xb, ya, yb = refs
    return [xa[i] for i in R3], [xb[i] for i in R3], ya[...], yb[...]


def apply_operator(field, around, diagonal, coupling):
    up_x, low_x, up_y, low_y = around
    nx = len(field[0])
    ny, nz = field[0][0].shape
    row = iota((ny, nz), 0)
    lane = iota((ny, nz), 1)
    result = [[None] * nx for _ in R3]
    for x in range(nx):
        own = [field[j][x] for j in R3]
        total = times(lambda i, j: diagonal[i, j, x], own)
        upper = [field[j][x + 1] if x + 1 < nx else up_x[j] for j in R3]
        part = times(lambda i, j: coupling[0, i, j, x], upper)
        total = [total[i] + part[i] for i in R3]
        if x:
            part = transposed_times(lambda i, j: coupling[0, i, j, x - 1], [field[j][x - 1] for j in R3])
        else:
            part = low_x
        total = [total[i] + part[i] for i in R3]
        upper = [jnp.where(row == ny - 1, up_y[j][x], pltpu.roll(own[j], ny - 1, 0)) for j in R3]
        part = times(lambda i, j: coupling[1, i, j, x], upper)
        total = [total[i] + part[i] for i in R3]
        part = transposed_times(lambda i, j: coupling[1, i, j, x], own)
        total = [total[i] + jnp.where(row == 0, low_y[i][x], pltpu.roll(part[i], 1, 0)) for i in R3]
        upper = [jnp.where(lane == nz - 1, 0.0, pltpu.roll(own[j], nz - 1, 1)) for j in R3]
        part = times(lambda i, j: coupling[2, i, j, x], upper)
        total = [total[i] + part[i] for i in R3]
        part = transposed_times(lambda i, j: coupling[2, i, j, x], own)
        total = [total[i] + jnp.where(lane == 0, 0.0, pltpu.roll(part[i], 1, 1)) for i in R3]
        for i in R3:
            result[i][x] = total[i]
    return result


def sweep(field, around, source, diagonal, coupling):
    image = apply_operator(field, around, diagonal, coupling)
    result = [[None] * len(field[0]) for _ in R3]
    for x in range(len(field[0])):
        defect = [source[i, x] - image[i][x] for i in R3]
        m = [[diagonal[i, j, x] for j in R3] for i in R3]
        adjugate = [
            [
                m[(j + 1) % 3][(i + 1) % 3] * m[(j + 2) % 3][(i + 2) % 3]
                - m[(j + 1) % 3][(i + 2) % 3] * m[(j + 2) % 3][(i + 1) % 3]
                for j in R3
            ]
            for i in R3
        ]
        determinant = m[0][0] * adjugate[0][0] + m[0][1] * adjugate[1][0] + m[0][2] * adjugate[2][0]
        change = times(lambda i, j: adjugate[i][j] / determinant, defect)
        for i in R3:
            result[i][x] = field[i][x] + damping * change[i]
    return result


def restrict(field, prolongator, aggregate, rows):
    nx = len(field[0])
    ny, nz = field[0][0].shape
    for x in range(nx):
        values = transposed_times(lambda i, j: prolongator[i, j, x], [field[j][x] for j in R3])
        for k in R3:
            high = values[k].astype(bf16).astype(f32)
            rest = values[k] - high
            middle = rest.astype(bf16).astype(f32)
            low = rest - middle
            for part, value in enumerate((high, middle, low)):
                rows[pl.ds(x * ny * 16 + 3 * part + k, ny, stride=16), :] = value
    which = iota((NA, nz), 0)
    total = None
    for first in range(0, nx * ny, 2):
        left, right = [], []
        for block in (first, first + 1):
            x, y = block // ny, block % ny
            left.append(rows[block * 16 : block * 16 + 16, :].astype(bf16))
            ids = jnp.broadcast_to(aggregate[x, y : y + 1, :], (NA, nz))
            right.append(jnp.where(ids == which, 1.0, 0.0).astype(bf16))
        part = lax.dot_general(
            jnp.concatenate(left, axis=1),
            jnp.concatenate(right, axis=1),
            (((1,), (1,)), ((), ())),
            preferred_element_type=f32,
        )
        total = part if total is None else total + part
    return [total[k : k + 1] + (total[3 + k : 4 + k] + total[6 + k : 7 + k]) for k in R3]


def prolong(coarse, prolongator, aggregate):
    nx, ny, nz = aggregate.shape
    tables = [jnp.broadcast_to(coarse[k], (ny, nz)) for k in R3]
    result = [[None] * nx for _ in R3]
    for x in range(nx):
        ids = aggregate[x]
        picked = [jnp.take_along_axis(tables[k], ids, axis=1, mode="promise_in_bounds") for k in R3]
        value = times(lambda i, j: prolongator[i, j, x], picked)
        for i in R3:
            result[i][x] = value[i]
    return result


def two_sum(a, b):
    s = a + b
    t = s - a
    return s, (a - (s - t)) + (b - t)


def quick_sum(a, b):
    s = a + b
    return s, b - (s - a)


def halves(a):
    c = 4097.0 * a
    high = c - (c - a)
    return high, a - high


def two_product(a, b):
    p = a * b
    ah, al = halves(a)
    bh, bl = halves(b)
    return p, ((ah * bh - p) + ah * bl + al * bh) + al * bl


def dd_add(x, y):
    s, e = two_sum(x[0], y[0])
    return quick_sum(s, e + (x[1] + y[1]))


def dd_neg(x):
    return -x[0], -x[1]


def dd_mul(x, y):
    p, e = two_product(x[0], y[0])
    return quick_sum(p, e + (x[0] * y[1] + x[1] * y[0]))


def dd_div(x, y):
    first = x[0] / y[0]
    rest = dd_add(x, dd_neg(dd_mul(y, (first, jnp.zeros_like(first)))))
    return quick_sum(first, rest[0] / y[0])


def dd_total(terms):
    terms = list(terms)
    while len(terms) > 1:
        terms = [dd_add(*terms[k : k + 2]) if k + 1 < len(terms) else terms[k] for k in range(0, len(terms), 2)]
    return terms[0]


def power_of_two(x):
    scale = jnp.full_like(x, 2.0**-126)
    inverse = jnp.full_like(x, 2.0**126)
    for step in (64, 64, 64, 32, 16, 8, 4, 2, 1):
        larger = scale * 2.0**step
        take = (x >= larger) & (larger <= 2.0**126)
        scale = jnp.where(take, larger, scale)
        inverse = jnp.where(take, inverse * 2.0**-step, inverse)
    return scale, inverse


def faces_kernel(field, coupling, *sends):
    send_faces(load_field(field), coupling, sends)


def sweep_kernel(send, field, source, diagonal, coupling, *refs):
    received, refs = refs[:4], refs[4:]
    own = load_field(field)
    around = halos(read_halos(received), len(own[0]))
    new = sweep(own, around, source, diagonal, coupling)
    store_field(refs[0], new)
    if send:
        send_faces(new, coupling, refs[1:])


def residual_kernel(field, source, diagonal, coupling, prolongator, aggregate, *refs):
    received, (vectors, fine), sends, rows = refs[:4], refs[4:6], refs[6:10], refs[10]
    own = load_field(field)
    around = halos(read_halos(received), len(own[0]))
    image = apply_operator(own, around, diagonal, coupling)
    defect = [[source[i, x] - image[i][x] for x in range(len(own[0]))] for i in R3]
    coarse = restrict(defect, prolongator, aggregate, rows)
    row = iota((8, LANES), 0)
    for k in R3:
        vectors[k] = jnp.where(row == 0, coarse[k], 0.0)
    new = prolong(coarse, prolongator, aggregate)
    store_field(fine, new)
    send_faces(new, coupling, sends)


def krylov_kernel(step, fine_in, vectors_in, diagonal, coupling, prolongator, aggregate, *refs):
    received, (vectors, fine), sends, rows = refs[:4], refs[4:6], refs[6:10], refs[10]
    own = load_field(fine_in)
    around = halos(read_halos(received), len(own[0]))
    image = apply_operator(own, around, diagonal, coupling)
    coarse = restrict(image, prolongator, aggregate, rows)
    row = iota((8, LANES), 0)
    for k in R3:
        vectors[k] = jnp.where(row == step, coarse[k], vectors_in[k])
    new = prolong(coarse, prolongator, aggregate)
    store_field(fine, new)
    send_faces(new, coupling, sends)


def gram_kernel(step, fine_in, vectors_in, diagonal, coupling, prolongator, aggregate, *refs):
    received, payload, rows = refs[:4], refs[4], refs[5]
    own = load_field(fine_in)
    around = halos(read_halos(received), len(own[0]))
    image = apply_operator(own, around, diagonal, coupling)
    coarse = restrict(image, prolongator, aggregate, rows)
    shape = (8, LANES)
    row, lane = iota(shape, 0), iota(shape, 1)
    all_vectors = [jnp.where(row == step, coarse[k], vectors_in[k]) for k in R3]
    largest = jnp.maximum(jnp.maximum(jnp.abs(all_vectors[0]), jnp.abs(all_vectors[1])), jnp.abs(all_vectors[2]))
    largest = jnp.broadcast_to(jnp.max(largest, axis=1, keepdims=True), shape)
    scale, inverse = power_of_two(largest)
    unit = [all_vectors[k] * inverse for k in R3]
    out = jnp.zeros(shape, f32)
    for lag in range(KC + 1):
        other = [pltpu.roll(u, 8 - lag, 0) if lag else u for u in unit]
        total = dd_total([two_product(unit[k], other[k]) for k in R3])
        for by in (64, 32, 16, 8, 4, 2, 1):
            total = dd_add(total, tuple(pltpu.roll(t, by, 1) for t in total))
        scale_j, inverse_j = (pltpu.roll(s, 8 - lag, 0) if lag else s for s in (scale, inverse))
        pair = row + LAG_START[lag]
        here = row < LAG_COUNT[lag]
        for slot, value in enumerate((*total, scale, scale, scale_j, scale_j, inverse, inverse_j)):
            out = jnp.where(here & (lane == pair + 16 * slot), value, out)
    line = jnp.sum(out, axis=0, keepdims=True)
    payload[...] = jnp.broadcast_to(line, payload.shape)


def combine(gathered, vectors):
    n = gathered.shape[0]
    inverse = jnp.min(gathered[...], axis=0, keepdims=True)
    inverse_i = pltpu.roll(jnp.broadcast_to(inverse, (8, LANES)), 32, 1)
    inverse_j = pltpu.roll(jnp.broadcast_to(inverse, (8, LANES)), 16, 1)
    lane = iota((8, LANES), 1)
    inv_i = jnp.where(lane < 16, inverse_i, pltpu.roll(inverse_i, 16, 1))
    inv_j = jnp.where(lane < 16, inverse_j, pltpu.roll(inverse_j, 16, 1))
    terms = []
    for start in range(0, n, 8):
        block = gathered[start : start + 8, :]
        weight = (pltpu.roll(block, LANES - 32, 1) * inv_i) * (pltpu.roll(block, LANES - 64, 1) * inv_j)
        terms.append((jnp.where(lane < 32, block * weight, 0.0), jnp.zeros((8, LANES), f32)))
    total = dd_total(terms)
    for by in (4, 2, 1):
        total = dd_add(total, tuple(pltpu.roll(t, by, 0) for t in total))
    total = dd_add(total, (pltpu.roll(total[0], LANES - 16, 1), jnp.zeros((8, LANES), f32)))

    def spread(value, at):
        return jnp.broadcast_to(value[:, at : at + 1], (8, LANES))

    gram = {}
    for p, (i, j) in enumerate(PAIRS):
        gram[i, j] = gram[j, i] = (spread(total[0], p), spread(total[1], p))
    at_i = {i: p for p, (i, j) in enumerate(PAIRS) if j == i}
    unscale = [spread(inverse_i, at_i[i]) for i in range(KC)] + [spread(inverse_j, PAIRS.index((0, KC)))]
    scale0 = power_of_two(1.25 / unscale[0])[0]
    growth = [power_of_two(1.25 * unscale[j] / unscale[j + 1])[0] for j in range(KC)]
    zero = jnp.zeros((8, LANES), f32)
    one = jnp.ones((8, LANES), f32)
    residual = [(one, zero)]
    direction = [(one, zero)]
    answer = []
    rr = gram[0, 0]
    start = rr[0]
    for it in range(KC):
        image = [None] + [(growth[j] * d[0], growth[j] * d[1]) for j, d in enumerate(direction)]
        products = [
            dd_mul(direction[i], dd_total([dd_mul(gram[i, j], image[j]) for j in range(1, it + 2)])) for i in range(it + 1)
        ]
        curvature = dd_total(products)
        live = rr[0] > 1e-12 * start
        alpha = dd_div(rr, tuple(jnp.where(live, c, o) for c, o in zip(curvature, (one, zero))))
        alpha = tuple(jnp.where(live, a, 0.0) for a in alpha)
        steps = [dd_mul(alpha, d) for d in direction]
        answer = [dd_add(a, s) for a, s in zip(answer, steps)] + steps[len(answer) :]
        if it + 1 == KC:
            break
        moved = [None] + [dd_neg(dd_mul(alpha, image[j])) for j in range(1, it + 2)]
        residual = [residual[0]] + [
            dd_add(residual[j], moved[j]) if j < len(residual) else moved[j] for j in range(1, it + 2)
        ]
        products = [
            dd_mul(residual[i], dd_total([dd_mul(gram[i, j], residual[j]) for j in range(it + 2)])) for i in range(it + 2)
        ]
        new = dd_total(products)
        beta = dd_div(new, tuple(jnp.where(live, c, o) for c, o in zip(rr, (one, zero))))
        direction = [dd_add(residual[j], dd_mul(beta, direction[j])) for j in range(it + 1)] + residual[it + 1 :]
        rr = new
    return [a[0] * (scale0 * unscale[j]) for j, a in enumerate(answer)]


def correct_kernel(gathered, vectors, field, source, diagonal, coupling, prolongator, aggregate, *refs):
    received, refs = refs[: 4 * (KC + 1)], refs[4 * (KC + 1) :]
    correction, new_field, sends = refs[0], refs[1], refs[2:]
    weights = combine(gathered, vectors)
    coarse = []
    for k in R3:
        total = None
        for j in range(KC):
            part = weights[j][0:1] * vectors[k, j : j + 1, :]
            total = part if total is None else total + part
        coarse.append(total)
        correction[k] = total
    nx = field.shape[1]
    rise = prolong(coarse, prolongator, aggregate)
    own = [[field[c, x] + rise[c][x] for x in range(nx)] for c in R3]
    around = read_halos(received[:4])
    for j in range(KC):
        part = read_halos(received[4 * (j + 1) : 4 * (j + 2)])
        weight = weights[j]
        around = (
            [a + weight * b for a, b in zip(around[0], part[0])],
            [a + weight * b for a, b in zip(around[1], part[1])],
            around[2] + weight[0:1] * part[2],
            around[3] + weight[0:1] * part[3],
        )
    new = sweep(own, halos(around, nx), source, diagonal, coupling)
    store_field(new_field, new)
    send_faces(new, coupling, sends)


def call(kernel, out_shapes, inputs, scratch=()):
    return pl.pallas_call(
        kernel,
        out_shape=[jax.ShapeDtypeStruct(s, f32) for s in out_shapes],
        in_specs=[pl.BlockSpec(memory_space=VMEM)] * len(inputs),
        out_specs=[pl.BlockSpec(memory_space=VMEM)] * len(out_shapes),
        scratch_shapes=list(scratch),
        compiler_params=pltpu.CompilerParams(vmem_limit_bytes=16 * 2**20),
    )(*inputs)


def local(source, initial_guess, coupling, diagonal_block, prolongator, aggregate):
    _, nx, ny, nz = source.shape
    devices = lax.axis_size("sx") * lax.axis_size("sy")
    shape = source.shape
    send_shapes = [(3, ny, nz)] * 2 + [(3 * nx, nz)] * 2
    vector_shape = (3, 8, LANES)
    rows = [pltpu.VMEM((nx * ny * 16, nz), f32)]

    received = exchange(call(faces_kernel, send_shapes, (initial_guess, coupling)))
    field = initial_guess
    for _ in range(NU):
        field, *sends = call(
            functools.partial(sweep_kernel, True),
            [shape] + send_shapes,
            (field, source, diagonal_block, coupling, *received),
        )
        received = exchange(sends)
    smoothed, smoothed_halos = field, received
    vectors, fine, *sends = call(
        residual_kernel,
        [vector_shape, shape] + send_shapes,
        (smoothed, source, diagonal_block, coupling, prolongator, aggregate, *received),
        rows,
    )
    krylov_halos = [exchange(sends)]
    for step in range(1, KC):
        vectors, fine, *sends = call(
            functools.partial(krylov_kernel, step),
            [vector_shape, shape] + send_shapes,
            (fine, vectors, diagonal_block, coupling, prolongator, aggregate, *krylov_halos[-1]),
            rows,
        )
        krylov_halos.append(exchange(sends))
    (payload,) = call(
        functools.partial(gram_kernel, KC),
        [(devices, LANES)],
        (fine, vectors, diagonal_block, coupling, prolongator, aggregate, *krylov_halos[-1]),
        rows,
    )
    gathered = lax.all_to_all(payload.reshape(devices, 1, LANES), ("sx", "sy"), 0, 0).reshape(devices, LANES)
    correction, field, *sends = call(
        correct_kernel,
        [(3, 1, LANES), shape] + send_shapes,
        (gathered, vectors, smoothed, source, diagonal_block, coupling, prolongator, aggregate, *smoothed_halos)
        + tuple(h for halo in krylov_halos for h in halo),
    )
    for number in range(1, NU):
        last = number + 1 == NU
        field, *sends = call(
            functools.partial(sweep_kernel, not last),
            [shape] + ([] if last else send_shapes),
            (field, source, diagonal_block, coupling, *exchange(sends)),
        )
    return field, correction.reshape(3, 1, 1, NA)


def solution(mesh):
    in_specs = (
        P(None, "sx", "sy", None),
        P(None, "sx", "sy", None),
        P(None, None, None, "sx", "sy", None),
        P(None, None, "sx", "sy", None),
        P(None, None, "sx", "sy", None),
        P("sx", "sy", None),
    )
    out_specs = (P(None, "sx", "sy", None), P(None, "sx", "sy", None))
    return jax.shard_map(local, mesh=mesh, in_specs=in_specs, out_specs=out_specs, check_vma=False)
```

```python
import functools

import jax
import jax.numpy as jnp
from jax import lax
from jax.experimental import pallas as pl
from jax.experimental.pallas import tpu as pltpu
from jax.sharding import PartitionSpec as P

NU = 2
KC = 4
NA = 128
LANES = 128

damping = 0.8
R3 = range(3)
VMEM = pltpu.VMEM
f32 = jnp.float32
bf16 = jnp.bfloat16

PAIRS = [(i, i + lag) for lag in range(KC + 1) for i in range(KC) if i + lag <= KC]
LAG_START = [min(p for p, (i, j) in enumerate(PAIRS) if j - i == lag) for lag in range(KC + 1)]
LAG_COUNT = [sum(1 for i, j in PAIRS if j - i == lag) for lag in range(KC + 1)]


def pair_exchange(x, axis, odd):
    n = lax.axis_size(axis)
    if odd:
        pairs = [(k, (k + 1) % n) for k in range(1, n, 2)] + [((k + 1) % n, k) for k in range(1, n, 2)]
    else:
        pairs = [(k, k ^ 1) for k in range(n)]
    return lax.ppermute(x, axis, pairs)


def exchange(sends):
    yb, xb, ya, xa = sends
    return (
        pair_exchange(yb, "sy", True),
        pair_exchange(xb, "sx", True),
        pair_exchange(ya, "sy", False),
        pair_exchange(xa, "sx", False),
    )


def iota(shape, dim):
    return lax.broadcasted_iota(jnp.int32, shape, dim)


def sides(axis):
    index = lax.axis_index(axis)
    return index % 2 == 0, index == 0, index == lax.axis_size(axis) - 1


def load_field(ref):
    return [[ref[c, x] for x in range(ref.shape[1])] for c in R3]


def store_field(ref, field):
    for c in R3:
        for x in range(ref.shape[1]):
            ref[c, x] = field[c][x]


def times(block, vector):
    return [block(i, 0) * vector[0] + block(i, 1) * vector[1] + block(i, 2) * vector[2] for i in R3]


def transposed_times(block, vector):
    return [block(0, i) * vector[0] + block(1, i) * vector[1] + block(2, i) * vector[2] for i in R3]


def send_faces(fields, coupling, sends):
    yb, xb, ya, xa = sends
    nx = len(fields[0][0])
    ny = fields[0][0][0].shape[0]
    even_x, _, _ = sides("sx")
    even_y, _, _ = sides("sy")
    for number, field in enumerate(fields):
        for x in range(nx):
            top = transposed_times(
                lambda i, j: coupling[1, i, j, x, ny - 1 : ny], [field[j][x][ny - 1 : ny] for j in R3]
            )
            for i in R3:
                bottom = field[i][x][0:1]
                row = (3 * number + i) * nx + x
                ya[row : row + 1] = jnp.where(even_y, top[i], bottom)
                yb[row : row + 1] = jnp.where(even_y, bottom, top[i])
        top = transposed_times(lambda i, j: coupling[0, i, j, nx - 1], [field[j][nx - 1] for j in R3])
        for i in R3:
            bottom = field[i][0]
            xa[3 * number + i] = jnp.where(even_x, top[i], bottom)
            xb[3 * number + i] = jnp.where(even_x, bottom, top[i])


def halos(received, nx):
    xa, xb, ya, yb = received
    even_x, first_x, last_x = sides("sx")
    even_y, first_y, last_y = sides("sy")
    up_x = [jnp.where(last_x, 0.0, jnp.where(even_x, xa[i], xb[i])) for i in R3]
    low_x = [jnp.where(first_x, 0.0, jnp.where(even_x, xb[i], xa[i])) for i in R3]
    up_y = jnp.where(last_y, 0.0, jnp.where(even_y, ya, yb))
    low_y = jnp.where(first_y, 0.0, jnp.where(even_y, yb, ya))
    up_y = [[up_y[i * nx + x : i * nx + x + 1] for x in range(nx)] for i in R3]
    low_y = [[low_y[i * nx + x : i * nx + x + 1] for x in range(nx)] for i in R3]
    return up_x, low_x, up_y, low_y


def read_halos(refs, nx, number=0):
    yb, xb, ya, xa = refs
    at = 3 * number
    rows = slice(at * nx, (at + 3) * nx)
    return [xa[at + i] for i in R3], [xb[at + i] for i in R3], ya[rows], yb[rows]


def apply_operator(field, around, diagonal, coupling):
    up_x, low_x, up_y, low_y = around
    nx = len(field[0])
    ny, nz = field[0][0].shape
    row = iota((ny, nz), 0)
    lane = iota((ny, nz), 1)
    result = [[None] * nx for _ in R3]
    for x in range(nx):
        own = [field[j][x] for j in R3]
        total = times(lambda i, j: diagonal[i, j, x], own)
        upper = [field[j][x + 1] if x + 1 < nx else up_x[j] for j in R3]
        part = times(lambda i, j: coupling[0, i, j, x], upper)
        total = [total[i] + part[i] for i in R3]
        if x:
            part = transposed_times(lambda i, j: coupling[0, i, j, x - 1], [field[j][x - 1] for j in R3])
        else:
            part = low_x
        total = [total[i] + part[i] for i in R3]
        upper = [jnp.where(row == ny - 1, up_y[j][x], pltpu.roll(own[j], ny - 1, 0)) for j in R3]
        part = times(lambda i, j: coupling[1, i, j, x], upper)
        total = [total[i] + part[i] for i in R3]
        part = transposed_times(lambda i, j: coupling[1, i, j, x], own)
        total = [total[i] + jnp.where(row == 0, low_y[i][x], pltpu.roll(part[i], 1, 0)) for i in R3]
        upper = [jnp.where(lane == nz - 1, 0.0, pltpu.roll(own[j], nz - 1, 1)) for j in R3]
        part = times(lambda i, j: coupling[2, i, j, x], upper)
        total = [total[i] + part[i] for i in R3]
        part = transposed_times(lambda i, j: coupling[2, i, j, x], own)
        total = [total[i] + jnp.where(lane == 0, 0.0, pltpu.roll(part[i], 1, 1)) for i in R3]
        for i in R3:
            result[i][x] = total[i]
    return result


def relaxed(field, defect, diagonal):
    result = [[None] * len(field[0]) for _ in R3]
    for x in range(len(field[0])):
        m = [[diagonal[i, j, x] for j in R3] for i in R3]
        adjugate = [
            [
                m[(j + 1) % 3][(i + 1) % 3] * m[(j + 2) % 3][(i + 2) % 3]
                - m[(j + 1) % 3][(i + 2) % 3] * m[(j + 2) % 3][(i + 1) % 3]
                for j in R3
            ]
            for i in R3
        ]
        determinant = m[0][0] * adjugate[0][0] + m[0][1] * adjugate[1][0] + m[0][2] * adjugate[2][0]
        change = times(lambda i, j: adjugate[i][j] / determinant, [defect[i][x] for i in R3])
        for i in R3:
            result[i][x] = field[i][x] + damping * change[i]
    return result


def defect_of(source, image):
    return [[source[i, x] - image[i][x] for x in range(len(image[0]))] for i in R3]


def negated(image):
    return [[-value for value in row] for row in image]


def restrict(field, prolongator, aggregate, rows):
    nx = len(field[0])
    ny, nz = field[0][0].shape
    for x in range(nx):
        values = transposed_times(lambda i, j: prolongator[i, j, x], [field[j][x] for j in R3])
        for k in R3:
            high = values[k].astype(bf16).astype(f32)
            rest = values[k] - high
            middle = rest.astype(bf16).astype(f32)
            low = rest - middle
            for part, value in enumerate((high, middle, low)):
                rows[pl.ds(x * ny * 16 + 3 * part + k, ny, stride=16), :] = value
    which = iota((NA, nz), 0)
    total = None
    for first in range(0, nx * ny, 2):
        left, right = [], []
        for block in (first, first + 1):
            x, y = block // ny, block % ny
            left.append(rows[block * 16 : block * 16 + 16, :].astype(bf16))
            ids = jnp.broadcast_to(aggregate[x, y : y + 1, :], (NA, nz))
            right.append(jnp.where(ids == which, 1.0, 0.0).astype(bf16))
        part = lax.dot_general(
            jnp.concatenate(left, axis=1),
            jnp.concatenate(right, axis=1),
            (((1,), (1,)), ((), ())),
            preferred_element_type=f32,
        )
        total = part if total is None else total + part
    return [total[k : k + 1] + (total[3 + k : 4 + k] + total[6 + k : 7 + k]) for k in R3]


def prolong(coarse, prolongator, aggregate):
    nx, ny, nz = aggregate.shape
    tables = [jnp.broadcast_to(coarse[k], (ny, nz)) for k in R3]
    result = [[None] * nx for _ in R3]
    for x in range(nx):
        ids = aggregate[x]
        picked = [jnp.take_along_axis(tables[k], ids, axis=1, mode="promise_in_bounds") for k in R3]
        value = times(lambda i, j: prolongator[i, j, x], picked)
        for i in R3:
            result[i][x] = value[i]
    return result


def two_sum(a, b):
    s = a + b
    t = s - a
    return s, (a - (s - t)) + (b - t)


def quick_sum(a, b):
    s = a + b
    return s, b - (s - a)


def halves(a):
    c = 4097.0 * a
    high = c - (c - a)
    return high, a - high


def two_product(a, b):
    p = a * b
    ah, al = halves(a)
    bh, bl = halves(b)
    return p, ((ah * bh - p) + ah * bl + al * bh) + al * bl


def dd_add(x, y):
    s, e = two_sum(x[0], y[0])
    return quick_sum(s, e + (x[1] + y[1]))


def dd_neg(x):
    return -x[0], -x[1]


def dd_mul(x, y):
    p, e = two_product(x[0], y[0])
    return quick_sum(p, e + (x[0] * y[1] + x[1] * y[0]))


def dd_div(x, y):
    first = x[0] / y[0]
    rest = dd_add(x, dd_neg(dd_mul(y, (first, jnp.zeros_like(first)))))
    return quick_sum(first, rest[0] / y[0])


def dd_total(terms):
    terms = list(terms)
    while len(terms) > 1:
        terms = [dd_add(*terms[k : k + 2]) if k + 1 < len(terms) else terms[k] for k in range(0, len(terms), 2)]
    return terms[0]


def power_of_two(x):
    scale = jnp.full_like(x, 2.0**-126)
    inverse = jnp.full_like(x, 2.0**126)
    for step in (64, 64, 64, 32, 16, 8, 4, 2, 1):
        larger = scale * 2.0**step
        take = (x >= larger) & (larger <= 2.0**126)
        scale = jnp.where(take, larger, scale)
        inverse = jnp.where(take, inverse * 2.0**-step, inverse)
    return scale, inverse


def faces_kernel(field, coupling, *sends):
    send_faces([load_field(field)], coupling, sends)


def sweep_kernel(field, source, diagonal, coupling, *refs):
    received, new_field, sends = refs[:4], refs[4], refs[5:]
    own = load_field(field)
    nx = len(own[0])
    image = apply_operator(own, halos(read_halos(received, nx), nx), diagonal, coupling)
    new = relaxed(own, defect_of(source, image), diagonal)
    store_field(new_field, new)
    send_faces([new], coupling, sends)


def residual_kernel(field, source, diagonal, coupling, prolongator, aggregate, *refs):
    received, (vectors, fine, further), sends, rows = refs[:4], refs[4:7], refs[7:11], refs[11]
    own = load_field(field)
    nx = len(own[0])
    image = apply_operator(own, halos(read_halos(received, nx), nx), diagonal, coupling)
    defect = defect_of(source, image)
    coarse = restrict(defect, prolongator, aggregate, rows)
    row = iota((8, LANES), 0)
    for k in R3:
        vectors[k] = jnp.where(row == 0, coarse[k], 0.0)
    new = prolong(coarse, prolongator, aggregate)
    store_field(fine, new)
    swept = relaxed(own, defect, diagonal)
    store_field(further, swept)
    send_faces([new, swept], coupling, sends)


def krylov_kernel(step, fine_in, vectors_in, diagonal, coupling, prolongator, aggregate, *refs):
    received, (vectors, fine, further), sends, rows = refs[:4], refs[4:7], refs[7:11], refs[11]
    own = load_field(fine_in)
    nx = len(own[0])
    image = apply_operator(own, halos(read_halos(received, nx), nx), diagonal, coupling)
    coarse = restrict(image, prolongator, aggregate, rows)
    row = iota((8, LANES), 0)
    for k in R3:
        vectors[k] = jnp.where(row == step, coarse[k], vectors_in[k])
    new = prolong(coarse, prolongator, aggregate)
    store_field(fine, new)
    swept = relaxed(own, negated(image), diagonal)
    store_field(further, swept)
    send_faces([new, swept], coupling, sends)


def gram_kernel(step, fine_in, vectors_in, diagonal, coupling, prolongator, aggregate, *refs):
    received, payload, further, sends, rows = refs[:4], refs[4], refs[5], refs[6:10], refs[10]
    own = load_field(fine_in)
    nx = len(own[0])
    image = apply_operator(own, halos(read_halos(received, nx), nx), diagonal, coupling)
    swept = relaxed(own, negated(image), diagonal)
    store_field(further, swept)
    send_faces([swept], coupling, sends)
    coarse = restrict(image, prolongator, aggregate, rows)
    shape = (8, LANES)
    row, lane = iota(shape, 0), iota(shape, 1)
    all_vectors = [jnp.where(row == step, coarse[k], vectors_in[k]) for k in R3]
    largest = jnp.maximum(jnp.maximum(jnp.abs(all_vectors[0]), jnp.abs(all_vectors[1])), jnp.abs(all_vectors[2]))
    largest = jnp.broadcast_to(jnp.max(largest, axis=1, keepdims=True), shape)
    scale, inverse = power_of_two(largest)
    unit = [all_vectors[k] * inverse for k in R3]
    out = jnp.zeros(shape, f32)
    for lag in range(KC + 1):
        other = [pltpu.roll(u, 8 - lag, 0) if lag else u for u in unit]
        total = dd_total([two_product(unit[k], other[k]) for k in R3])
        for by in (64, 32, 16, 8, 4, 2, 1):
            total = dd_add(total, tuple(pltpu.roll(t, by, 1) for t in total))
        scale_j, inverse_j = (pltpu.roll(s, 8 - lag, 0) if lag else s for s in (scale, inverse))
        pair = row + LAG_START[lag]
        here = row < LAG_COUNT[lag]
        for slot, value in enumerate((*total, scale, scale, scale_j, scale_j, inverse, inverse_j)):
            out = jnp.where(here & (lane == pair + 16 * slot), value, out)
    line = jnp.sum(out, axis=0, keepdims=True)
    payload[...] = jnp.broadcast_to(line, payload.shape)


def combine(gathered):
    n = gathered.shape[0]
    inverse = jnp.min(gathered[...], axis=0, keepdims=True)
    inverse_i = pltpu.roll(jnp.broadcast_to(inverse, (8, LANES)), 32, 1)
    inverse_j = pltpu.roll(jnp.broadcast_to(inverse, (8, LANES)), 16, 1)
    lane = iota((8, LANES), 1)
    inv_i = jnp.where(lane < 16, inverse_i, pltpu.roll(inverse_i, 16, 1))
    inv_j = jnp.where(lane < 16, inverse_j, pltpu.roll(inverse_j, 16, 1))
    terms = []
    for start in range(0, n, 8):
        block = gathered[start : start + 8, :]
        weight = (pltpu.roll(block, LANES - 32, 1) * inv_i) * (pltpu.roll(block, LANES - 64, 1) * inv_j)
        terms.append((jnp.where(lane < 32, block * weight, 0.0), jnp.zeros((8, LANES), f32)))
    total = dd_total(terms)
    for by in (4, 2, 1):
        total = dd_add(total, tuple(pltpu.roll(t, by, 0) for t in total))
    total = dd_add(total, (pltpu.roll(total[0], LANES - 16, 1), jnp.zeros((8, LANES), f32)))

    def spread(value, at):
        return jnp.broadcast_to(value[:, at : at + 1], (8, LANES))

    gram = {}
    for p, (i, j) in enumerate(PAIRS):
        gram[i, j] = gram[j, i] = (spread(total[0], p), spread(total[1], p))
    at_i = {i: p for p, (i, j) in enumerate(PAIRS) if j == i}
    unscale = [spread(inverse_i, at_i[i]) for i in range(KC)] + [spread(inverse_j, PAIRS.index((0, KC)))]
    scale0 = power_of_two(1.25 / unscale[0])[0]
    growth = [power_of_two(1.25 * unscale[j] / unscale[j + 1])[0] for j in range(KC)]
    zero = jnp.zeros((8, LANES), f32)
    one = jnp.ones((8, LANES), f32)
    residual = [(one, zero)]
    direction = [(one, zero)]
    answer = []
    rr = gram[0, 0]
    start = rr[0]
    for it in range(KC):
        image = [None] + [(growth[j] * d[0], growth[j] * d[1]) for j, d in enumerate(direction)]
        products = [
            dd_mul(direction[i], dd_total([dd_mul(gram[i, j], image[j]) for j in range(1, it + 2)])) for i in range(it + 1)
        ]
        curvature = dd_total(products)
        live = rr[0] > 1e-12 * start
        alpha = dd_div(rr, tuple(jnp.where(live, c, o) for c, o in zip(curvature, (one, zero))))
        alpha = tuple(jnp.where(live, a, 0.0) for a in alpha)
        steps = [dd_mul(alpha, d) for d in direction]
        answer = [dd_add(a, s) for a, s in zip(answer, steps)] + steps[len(answer) :]
        if it + 1 == KC:
            break
        moved = [None] + [dd_neg(dd_mul(alpha, image[j])) for j in range(1, it + 2)]
        residual = [residual[0]] + [
            dd_add(residual[j], moved[j]) if j < len(residual) else moved[j] for j in range(1, it + 2)
        ]
        products = [
            dd_mul(residual[i], dd_total([dd_mul(gram[i, j], residual[j]) for j in range(it + 2)])) for i in range(it + 2)
        ]
        new = dd_total(products)
        beta = dd_div(new, tuple(jnp.where(live, c, o) for c, o in zip(rr, (one, zero))))
        direction = [dd_add(residual[j], dd_mul(beta, direction[j])) for j in range(it + 1)] + residual[it + 1 :]
        rr = new
    return [a[0] * (scale0 * unscale[j]) for j, a in enumerate(answer)]


def finish_kernel(gathered, vectors, source, diagonal, coupling, *refs):
    parts, refs = refs[: KC + 1], refs[KC + 1 :]
    received, (correction, new_field) = refs[: 4 * (KC + 1)], refs[4 * (KC + 1) :]
    weights = combine(gathered)
    for k in R3:
        total = None
        for j in range(KC):
            part = weights[j][0:1] * vectors[k, j : j + 1, :]
            total = part if total is None else total + part
        correction[k] = total
    own = load_field(parts[0])
    nx = len(own[0])
    around = read_halos(received[:4], nx, 1)
    for j in range(KC):
        weight = weights[j]
        own = [[own[c][x] + weight * parts[j + 1][c, x] for x in range(nx)] for c in R3]
        part = read_halos(received[4 * (j + 1) : 4 * (j + 2)], nx, 1 if j + 1 < KC else 0)
        around = (
            [a + weight * b for a, b in zip(around[0], part[0])],
            [a + weight * b for a, b in zip(around[1], part[1])],
            around[2] + weight[0:1] * part[2],
            around[3] + weight[0:1] * part[3],
        )
    image = apply_operator(own, halos(around, nx), diagonal, coupling)
    store_field(new_field, relaxed(own, defect_of(source, image), diagonal))


def call(kernel, out_shapes, inputs, scratch=()):
    return pl.pallas_call(
        kernel,
        out_shape=[jax.ShapeDtypeStruct(s, f32) for s in out_shapes],
        in_specs=[pl.BlockSpec(memory_space=VMEM)] * len(inputs),
        out_specs=[pl.BlockSpec(memory_space=VMEM)] * len(out_shapes),
        scratch_shapes=list(scratch),
        compiler_params=pltpu.CompilerParams(vmem_limit_bytes=16 * 2**20),
    )(*inputs)


def local(source, initial_guess, coupling, diagonal_block, prolongator, aggregate):
    _, nx, ny, nz = source.shape
    devices = lax.axis_size("sx") * lax.axis_size("sy")
    shape = source.shape
    vector_shape = (3, 8, LANES)
    rows = [pltpu.VMEM((nx * ny * 16, nz), f32)]

    def send_shapes(fields):
        faces, lines = (3 * fields, ny, nz), (3 * fields * ny, nz)
        return [lines, faces, lines, faces]

    received = exchange(call(faces_kernel, send_shapes(1), (initial_guess, coupling)))
    field = initial_guess
    for _ in range(NU):
        field, *sends = call(
            sweep_kernel, [shape] + send_shapes(1), (field, source, diagonal_block, coupling, *received)
        )
        received = exchange(sends)
    vectors, fine, further, *sends = call(
        residual_kernel,
        [vector_shape, shape, shape] + send_shapes(2),
        (field, source, diagonal_block, coupling, prolongator, aggregate, *received),
        rows,
    )
    parts, around = [further], [exchange(sends)]
    for step in range(1, KC):
        vectors, fine, further, *sends = call(
            functools.partial(krylov_kernel, step),
            [vector_shape, shape, shape] + send_shapes(2),
            (fine, vectors, diagonal_block, coupling, prolongator, aggregate, *around[-1]),
            rows,
        )
        parts.append(further)
        around.append(exchange(sends))
    payload, further, *sends = call(
        functools.partial(gram_kernel, KC),
        [(devices, LANES), shape] + send_shapes(1),
        (fine, vectors, diagonal_block, coupling, prolongator, aggregate, *around[-1]),
        rows,
    )
    parts.append(further)
    around.append(exchange(sends))
    gathered = lax.all_to_all(payload.reshape(devices, 1, LANES), ("sx", "sy"), 0, 0).reshape(devices, LANES)
    correction, field = call(
        finish_kernel,
        [(3, 1, LANES), shape],
        (gathered, vectors, source, diagonal_block, coupling, *parts) + tuple(h for halo in around for h in halo),
    )
    return field, correction.reshape(3, 1, 1, NA)


def solution(mesh):
    in_specs = (
        P(None, "sx", "sy", None),
        P(None, "sx", "sy", None),
        P(None, None, None, "sx", "sy", None),
        P(None, None, "sx", "sy", None),
        P(None, None, "sx", "sy", None),
        P("sx", "sy", None),
    )
    out_specs = (P(None, "sx", "sy", None), P(None, "sx", "sy", None))
    return jax.shard_map(local, mesh=mesh, in_specs=in_specs, out_specs=out_specs, check_vma=False)
```

```python
import functools

import jax
import jax.numpy as jnp
from jax import lax
from jax.experimental import pallas as pl
from jax.experimental.pallas import tpu as pltpu
from jax.sharding import PartitionSpec as P

NU = 2
KC = 4
NA = 128
LANES = 128

damping = 0.8
R3 = range(3)
VMEM = pltpu.VMEM
f32 = jnp.float32
bf16 = jnp.bfloat16

PAIRS = [(i, i + lag) for lag in range(KC + 1) for i in range(KC) if i + lag <= KC]
LAG_START = [min(p for p, (i, j) in enumerate(PAIRS) if j - i == lag) for lag in range(KC + 1)]
LAG_COUNT = [sum(1 for i, j in PAIRS if j - i == lag) for lag in range(KC + 1)]


def pair_exchange(x, axis, odd):
    n = lax.axis_size(axis)
    if odd:
        pairs = [(k, (k + 1) % n) for k in range(1, n, 2)] + [((k + 1) % n, k) for k in range(1, n, 2)]
    else:
        pairs = [(k, k ^ 1) for k in range(n)]
    return lax.ppermute(x, axis, pairs)


def exchange(sends):
    yb, xb, ya, xa = sends
    return (
        pair_exchange(yb, "sy", True),
        pair_exchange(xb, "sx", True),
        pair_exchange(ya, "sy", False),
        pair_exchange(xa, "sx", False),
    )


def iota(shape, dim):
    return lax.broadcasted_iota(jnp.int32, shape, dim)


def sides(axis):
    index = lax.axis_index(axis)
    return index % 2 == 0, index == 0, index == lax.axis_size(axis) - 1


def load_field(ref):
    return [[ref[c, x] for x in range(ref.shape[1])] for c in R3]


def store_field(ref, field):
    for c in R3:
        for x in range(ref.shape[1]):
            ref[c, x] = field[c][x]


def times(block, vector):
    return [block(i, 0) * vector[0] + block(i, 1) * vector[1] + block(i, 2) * vector[2] for i in R3]


def transposed_times(block, vector):
    return [block(0, i) * vector[0] + block(1, i) * vector[1] + block(2, i) * vector[2] for i in R3]


def send_faces(fields, coupling, sends):
    yb, xb, ya, xa = sends
    nx = len(fields[0][0])
    ny = fields[0][0][0].shape[0]
    even_x, _, _ = sides("sx")
    even_y, _, _ = sides("sy")
    for number, field in enumerate(fields):
        for x in range(nx):
            top = transposed_times(
                lambda i, j: coupling[1, i, j, x, ny - 1 : ny], [field[j][x][ny - 1 : ny] for j in R3]
            )
            for i in R3:
                bottom = field[i][x][0:1]
                row = (3 * number + i) * nx + x
                ya[row : row + 1] = jnp.where(even_y, top[i], bottom)
                yb[row : row + 1] = jnp.where(even_y, bottom, top[i])
        top = transposed_times(lambda i, j: coupling[0, i, j, nx - 1], [field[j][nx - 1] for j in R3])
        for i in R3:
            bottom = field[i][0]
            xa[3 * number + i] = jnp.where(even_x, top[i], bottom)
            xb[3 * number + i] = jnp.where(even_x, bottom, top[i])


def halos(received, nx):
    xa, xb, ya, yb = received
    even_x, first_x, last_x = sides("sx")
    even_y, first_y, last_y = sides("sy")
    up_x = [jnp.where(last_x, 0.0, jnp.where(even_x, xa[i], xb[i])) for i in R3]
    low_x = [jnp.where(first_x, 0.0, jnp.where(even_x, xb[i], xa[i])) for i in R3]
    up_y = jnp.where(last_y, 0.0, jnp.where(even_y, ya, yb))
    low_y = jnp.where(first_y, 0.0, jnp.where(even_y, yb, ya))
    up_y = [[up_y[i * nx + x : i * nx + x + 1] for x in range(nx)] for i in R3]
    low_y = [[low_y[i * nx + x : i * nx + x + 1] for x in range(nx)] for i in R3]
    return up_x, low_x, up_y, low_y


def read_halos(refs, nx, number=0):
    yb, xb, ya, xa = refs
    at = 3 * number
    rows = slice(at * nx, (at + 3) * nx)
    return [xa[at + i] for i in R3], [xb[at + i] for i in R3], ya[rows], yb[rows]


def apply_operator(field, around, diagonal, coupling):
    up_x, low_x, up_y, low_y = around
    nx = len(field[0])
    ny, nz = field[0][0].shape
    row = iota((ny, nz), 0)
    lane = iota((ny, nz), 1)
    result = [[None] * nx for _ in R3]
    for x in range(nx):
        own = [field[j][x] for j in R3]
        total = times(lambda i, j: diagonal[i, j, x], own)
        upper = [field[j][x + 1] if x + 1 < nx else up_x[j] for j in R3]
        part = times(lambda i, j: coupling[0, i, j, x], upper)
        total = [total[i] + part[i] for i in R3]
        if x:
            part = transposed_times(lambda i, j: coupling[0, i, j, x - 1], [field[j][x - 1] for j in R3])
        else:
            part = low_x
        total = [total[i] + part[i] for i in R3]
        upper = [jnp.where(row == ny - 1, up_y[j][x], pltpu.roll(own[j], ny - 1, 0)) for j in R3]
        part = times(lambda i, j: coupling[1, i, j, x], upper)
        total = [total[i] + part[i] for i in R3]
        part = transposed_times(lambda i, j: coupling[1, i, j, x], own)
        total = [total[i] + jnp.where(row == 0, low_y[i][x], pltpu.roll(part[i], 1, 0)) for i in R3]
        upper = [jnp.where(lane == nz - 1, 0.0, pltpu.roll(own[j], nz - 1, 1)) for j in R3]
        part = times(lambda i, j: coupling[2, i, j, x], upper)
        total = [total[i] + part[i] for i in R3]
        part = transposed_times(lambda i, j: coupling[2, i, j, x], own)
        total = [total[i] + jnp.where(lane == 0, 0.0, pltpu.roll(part[i], 1, 1)) for i in R3]
        for i in R3:
            result[i][x] = total[i]
    return result


def inverse_of(diagonal, x):
    m = [[diagonal[i, j, x] for j in R3] for i in R3]
    adjugate = [
        [
            m[(j + 1) % 3][(i + 1) % 3] * m[(j + 2) % 3][(i + 2) % 3]
            - m[(j + 1) % 3][(i + 2) % 3] * m[(j + 2) % 3][(i + 1) % 3]
            for j in R3
        ]
        for i in R3
    ]
    determinant = m[0][0] * adjugate[0][0] + m[0][1] * adjugate[1][0] + m[0][2] * adjugate[2][0]
    return [[adjugate[i][j] / determinant for j in R3] for i in R3]


def relaxed(field, defect, inverse):
    result = [[None] * len(field[0]) for _ in R3]
    for x in range(len(field[0])):
        change = times(lambda i, j: inverse[i, j, x], [defect[i][x] for i in R3])
        for i in R3:
            result[i][x] = field[i][x] + damping * change[i]
    return result


def defect_of(source, image):
    return [[source[i, x] - image[i][x] for x in range(len(image[0]))] for i in R3]


def negated(image):
    return [[-value for value in row] for row in image]


def restrict(field, prolongator, aggregate, rows):
    nx = len(field[0])
    ny, nz = field[0][0].shape
    for x in range(nx):
        values = transposed_times(lambda i, j: prolongator[i, j, x], [field[j][x] for j in R3])
        for k in R3:
            high = values[k].astype(bf16).astype(f32)
            rest = values[k] - high
            middle = rest.astype(bf16).astype(f32)
            low = rest - middle
            for part, value in enumerate((high, middle, low)):
                rows[pl.ds(x * ny * 16 + 3 * part + k, ny, stride=16), :] = value
    which = iota((NA, nz), 0)
    total = None
    for first in range(0, nx * ny, 2):
        left, right = [], []
        for block in (first, first + 1):
            x, y = block // ny, block % ny
            left.append(rows[block * 16 : block * 16 + 16, :].astype(bf16))
            ids = jnp.broadcast_to(aggregate[x, y : y + 1, :], (NA, nz))
            right.append(jnp.where(ids == which, 1.0, 0.0).astype(bf16))
        part = lax.dot_general(
            jnp.concatenate(left, axis=1),
            jnp.concatenate(right, axis=1),
            (((1,), (1,)), ((), ())),
            preferred_element_type=f32,
        )
        total = part if total is None else total + part
    return [total[k : k + 1] + (total[3 + k : 4 + k] + total[6 + k : 7 + k]) for k in R3]


def prolong(coarse, prolongator, aggregate):
    nx, ny, nz = aggregate.shape
    tables = [jnp.broadcast_to(coarse[k], (ny, nz)) for k in R3]
    result = [[None] * nx for _ in R3]
    for x in range(nx):
        ids = aggregate[x]
        picked = [jnp.take_along_axis(tables[k], ids, axis=1, mode="promise_in_bounds") for k in R3]
        value = times(lambda i, j: prolongator[i, j, x], picked)
        for i in R3:
            result[i][x] = value[i]
    return result


def two_sum(a, b):
    s = a + b
    t = s - a
    return s, (a - (s - t)) + (b - t)


def quick_sum(a, b):
    s = a + b
    return s, b - (s - a)


def halves(a):
    c = 4097.0 * a
    high = c - (c - a)
    return high, a - high


def two_product(a, b):
    p = a * b
    ah, al = halves(a)
    bh, bl = halves(b)
    return p, ((ah * bh - p) + ah * bl + al * bh) + al * bl


def dd_add(x, y):
    s, e = two_sum(x[0], y[0])
    return quick_sum(s, e + (x[1] + y[1]))


def dd_neg(x):
    return -x[0], -x[1]


def dd_mul(x, y):
    p, e = two_product(x[0], y[0])
    return p, e + (x[0] * y[1] + x[1] * y[0])


def dd_div(x, y, inverse):
    first = x[0] * inverse
    p, e = two_product(first, y[0])
    rest = ((x[0] - p) - e) + (x[1] - first * y[1])
    return quick_sum(first, rest * inverse)


def plain_total(terms):
    while len(terms) > 1:
        terms = [terms[k] + terms[k + 1] if k + 1 < len(terms) else terms[k] for k in range(0, len(terms), 2)]
    return terms[0]


def dd_total(terms):
    highs, lows = [t[0] for t in terms], [plain_total([t[1] for t in terms])]
    while len(highs) > 1:
        pairs = [two_sum(highs[k], highs[k + 1]) for k in range(0, len(highs) - 1, 2)]
        lows += [e for _, e in pairs]
        highs = [s for s, _ in pairs] + highs[2 * len(pairs) :]
    return quick_sum(highs[0], plain_total(lows))


def limbs(total):
    first = (total[0] + 1536.0) - 1536.0
    rest = total[0] - first
    second = (rest + 1.5 * 2.0**-7) - 1.5 * 2.0**-7
    return first, second, (rest - second) + total[1]


def power_of_two(x):
    scale = jnp.full_like(x, 2.0**-126)
    inverse = jnp.full_like(x, 2.0**126)
    for step in (64, 64, 64, 32, 16, 8, 4, 2, 1):
        larger = scale * 2.0**step
        take = (x >= larger) & (larger <= 2.0**126)
        scale = jnp.where(take, larger, scale)
        inverse = jnp.where(take, inverse * 2.0**-step, inverse)
    return scale, inverse


def inverse_kernel(diagonal, inverse):
    for x in range(diagonal.shape[2]):
        block = inverse_of(diagonal, x)
        for i in R3:
            for j in R3:
                inverse[i, j, x] = block[i][j]


def faces_kernel(field, coupling, *sends):
    send_faces([load_field(field)], coupling, sends)


def sweep_kernel(field, source, inverse, diagonal, coupling, *refs):
    received, new_field, sends = refs[:4], refs[4], refs[5:]
    own = load_field(field)
    nx = len(own[0])
    image = apply_operator(own, halos(read_halos(received, nx), nx), diagonal, coupling)
    new = relaxed(own, defect_of(source, image), inverse)
    store_field(new_field, new)
    send_faces([new], coupling, sends)


def residual_kernel(field, source, inverse, diagonal, coupling, prolongator, aggregate, *refs):
    received, (vectors, fine, further), sends, rows = refs[:4], refs[4:7], refs[7:11], refs[11]
    own = load_field(field)
    nx = len(own[0])
    image = apply_operator(own, halos(read_halos(received, nx), nx), diagonal, coupling)
    defect = defect_of(source, image)
    coarse = restrict(defect, prolongator, aggregate, rows)
    row = iota((8, LANES), 0)
    for k in R3:
        vectors[k] = jnp.where(row == 0, coarse[k], 0.0)
    new = prolong(coarse, prolongator, aggregate)
    store_field(fine, new)
    swept = relaxed(own, defect, inverse)
    store_field(further, swept)
    send_faces([new, swept], coupling, sends)


def krylov_kernel(step, fine_in, vectors_in, inverse, diagonal, coupling, prolongator, aggregate, *refs):
    received, (vectors, fine, further), sends, rows = refs[:4], refs[4:7], refs[7:11], refs[11]
    own = load_field(fine_in)
    nx = len(own[0])
    image = apply_operator(own, halos(read_halos(received, nx), nx), diagonal, coupling)
    coarse = restrict(image, prolongator, aggregate, rows)
    row = iota((8, LANES), 0)
    for k in R3:
        vectors[k] = jnp.where(row == step, coarse[k], vectors_in[k])
    new = prolong(coarse, prolongator, aggregate)
    store_field(fine, new)
    swept = relaxed(own, negated(image), inverse)
    store_field(further, swept)
    send_faces([new, swept], coupling, sends)


def gram_kernel(step, fine_in, vectors_in, inverse, diagonal, coupling, prolongator, aggregate, *refs):
    received, payload, further, sends, rows = refs[:4], refs[4], refs[5], refs[6:10], refs[10]
    own = load_field(fine_in)
    nx = len(own[0])
    image = apply_operator(own, halos(read_halos(received, nx), nx), diagonal, coupling)
    swept = relaxed(own, negated(image), inverse)
    store_field(further, swept)
    send_faces([swept], coupling, sends)
    coarse = restrict(image, prolongator, aggregate, rows)
    shape = (8, LANES)
    row, lane = iota(shape, 0), iota(shape, 1)
    all_vectors = [jnp.where(row == step, coarse[k], vectors_in[k]) for k in R3]
    largest = jnp.maximum(jnp.maximum(jnp.abs(all_vectors[0]), jnp.abs(all_vectors[1])), jnp.abs(all_vectors[2]))
    largest = jnp.broadcast_to(jnp.max(largest, axis=1, keepdims=True), shape)
    scale, inverse = power_of_two(largest)
    unit = [all_vectors[k] * inverse for k in R3]
    out = jnp.zeros(shape, f32)
    for lag in range(KC + 1):
        other = [pltpu.roll(u, 8 - lag, 0) if lag else u for u in unit]
        total = dd_total([two_product(unit[k], other[k]) for k in R3])
        sums = [jnp.broadcast_to(jnp.sum(part, axis=1, keepdims=True), shape) for part in limbs(total)]
        total = two_sum(sums[0], sums[1])
        total = quick_sum(total[0], total[1] + sums[2])
        scale_j, inverse_j = (pltpu.roll(s, 8 - lag, 0) if lag else s for s in (scale, inverse))
        pair = row + LAG_START[lag]
        here = row < LAG_COUNT[lag]
        for slot, value in enumerate((*total, scale, scale, scale_j, scale_j, inverse, inverse_j)):
            out = jnp.where(here & (lane == pair + 16 * slot), value, out)
    line = jnp.sum(out, axis=0, keepdims=True)
    payload[...] = jnp.broadcast_to(line, payload.shape)


def combine(gathered):
    n = gathered.shape[0]
    inverse = jnp.min(gathered[...], axis=0, keepdims=True)
    inverse_i = pltpu.roll(jnp.broadcast_to(inverse, (8, LANES)), 32, 1)
    inverse_j = pltpu.roll(jnp.broadcast_to(inverse, (8, LANES)), 16, 1)
    lane = iota((8, LANES), 1)
    inv_i = jnp.where(lane < 16, inverse_i, pltpu.roll(inverse_i, 16, 1))
    inv_j = jnp.where(lane < 16, inverse_j, pltpu.roll(inverse_j, 16, 1))
    terms = []
    for start in range(0, n, 8):
        block = gathered[start : start + 8, :]
        weight = (pltpu.roll(block, LANES - 32, 1) * inv_i) * (pltpu.roll(block, LANES - 64, 1) * inv_j)
        terms.append((jnp.where(lane < 32, block * weight, 0.0), jnp.zeros((8, LANES), f32)))
    total = dd_total(terms)
    for by in (4, 2, 1):
        total = dd_add(total, tuple(pltpu.roll(t, by, 0) for t in total))
    total = dd_add(total, (pltpu.roll(total[0], LANES - 16, 1), jnp.zeros((8, LANES), f32)))

    def spread(value, at):
        return jnp.broadcast_to(value[:, at : at + 1], (8, LANES))

    gram = {}
    for p, (i, j) in enumerate(PAIRS):
        gram[i, j] = gram[j, i] = (spread(total[0], p), spread(total[1], p))
    at_i = {i: p for p, (i, j) in enumerate(PAIRS) if j == i}
    unscale = [spread(inverse_i, at_i[i]) for i in range(KC)] + [spread(inverse_j, PAIRS.index((0, KC)))]
    scale0 = power_of_two(1.25 / unscale[0])[0]
    growth = [power_of_two(1.25 * unscale[j] / unscale[j + 1])[0] for j in range(KC)]
    zero = jnp.zeros((8, LANES), f32)
    one = jnp.ones((8, LANES), f32)
    residual = [(one, zero)]
    direction = [(one, zero)]
    answer = []
    rr = gram[0, 0]
    start = rr[0]
    inverse_rr = 1.0 / rr[0]
    for it in range(KC):
        image = [None] + [(growth[j] * d[0], growth[j] * d[1]) for j, d in enumerate(direction)]
        last = it + 1 == KC
        rows = [
            dd_total([dd_mul(gram[i, j], image[j]) for j in range(1, it + 2)]) for i in range(it + 1 if last else it + 2)
        ]
        curvature = dd_total([dd_mul(direction[i], rows[i]) for i in range(it + 1)])
        live = rr[0] > 1e-12 * start
        curvature = tuple(jnp.where(live, c, o) for c, o in zip(curvature, (one, zero)))
        alpha = dd_div(rr, curvature, 1.0 / curvature[0])
        alpha = tuple(jnp.where(live, a, 0.0) for a in alpha)
        steps = [dd_mul(alpha, d) for d in direction]
        answer = [dd_add(a, s) for a, s in zip(answer, steps)] + steps[len(answer) :]
        if last:
            break
        square = dd_total([dd_mul(image[i], rows[i]) for i in range(1, it + 2)])
        new = dd_add(dd_mul(quick_sum(*dd_mul(alpha, alpha)), square), dd_neg(rr))
        new = tuple(jnp.where(live, n, 0.0) for n in new)
        moved = [None] + [dd_neg(dd_mul(alpha, image[j])) for j in range(1, it + 2)]
        residual = [residual[0]] + [
            dd_add(residual[j], moved[j]) if j < len(residual) else quick_sum(*moved[j]) for j in range(1, it + 2)
        ]
        beta = dd_div(new, rr, inverse_rr)
        direction = [dd_add(residual[j], dd_mul(beta, direction[j])) for j in range(it + 1)] + residual[it + 1 :]
        rr = new
        inverse_rr = 1.0 / jnp.where(rr[0] > 0.0, rr[0], 1.0)
    return [a[0] * (scale0 * unscale[j]) for j, a in enumerate(answer)]


def finish_kernel(gathered, vectors, source, inverse, diagonal, coupling, *refs):
    parts, refs = refs[: KC + 1], refs[KC + 1 :]
    received, (correction, new_field) = refs[: 4 * (KC + 1)], refs[4 * (KC + 1) :]
    weights = combine(gathered)
    for k in R3:
        total = None
        for j in range(KC):
            part = weights[j][0:1] * vectors[k, j : j + 1, :]
            total = part if total is None else total + part
        correction[k] = total
    own = load_field(parts[0])
    nx = len(own[0])
    around = read_halos(received[:4], nx, 1)
    for j in range(KC):
        weight = weights[j]
        own = [[own[c][x] + weight * parts[j + 1][c, x] for x in range(nx)] for c in R3]
        part = read_halos(received[4 * (j + 1) : 4 * (j + 2)], nx, 1 if j + 1 < KC else 0)
        around = (
            [a + weight * b for a, b in zip(around[0], part[0])],
            [a + weight * b for a, b in zip(around[1], part[1])],
            around[2] + weight[0:1] * part[2],
            around[3] + weight[0:1] * part[3],
        )
    image = apply_operator(own, halos(around, nx), diagonal, coupling)
    store_field(new_field, relaxed(own, defect_of(source, image), inverse))


def call(kernel, out_shapes, inputs, scratch=()):
    return pl.pallas_call(
        kernel,
        out_shape=[jax.ShapeDtypeStruct(s, f32) for s in out_shapes],
        in_specs=[pl.BlockSpec(memory_space=VMEM)] * len(inputs),
        out_specs=[pl.BlockSpec(memory_space=VMEM)] * len(out_shapes),
        scratch_shapes=list(scratch),
        compiler_params=pltpu.CompilerParams(vmem_limit_bytes=16 * 2**20),
    )(*inputs)


def local(source, initial_guess, coupling, diagonal_block, prolongator, aggregate):
    _, nx, ny, nz = source.shape
    devices = lax.axis_size("sx") * lax.axis_size("sy")
    shape = source.shape
    vector_shape = (3, 8, LANES)
    rows = [pltpu.VMEM((nx * ny * 16, nz), f32)]

    def send_shapes(fields):
        faces, lines = (3 * fields, ny, nz), (3 * fields * ny, nz)
        return [lines, faces, lines, faces]

    received = exchange(call(faces_kernel, send_shapes(1), (initial_guess, coupling)))
    (inverse,) = call(inverse_kernel, [diagonal_block.shape], (diagonal_block,))
    field = initial_guess
    for _ in range(NU):
        field, *sends = call(
            sweep_kernel, [shape] + send_shapes(1), (field, source, inverse, diagonal_block, coupling, *received)
        )
        received = exchange(sends)
    vectors, fine, further, *sends = call(
        residual_kernel,
        [vector_shape, shape, shape] + send_shapes(2),
        (field, source, inverse, diagonal_block, coupling, prolongator, aggregate, *received),
        rows,
    )
    parts, around = [further], [exchange(sends)]
    for step in range(1, KC):
        vectors, fine, further, *sends = call(
            functools.partial(krylov_kernel, step),
            [vector_shape, shape, shape] + send_shapes(2),
            (fine, vectors, inverse, diagonal_block, coupling, prolongator, aggregate, *around[-1]),
            rows,
        )
        parts.append(further)
        around.append(exchange(sends))
    payload, further, *sends = call(
        functools.partial(gram_kernel, KC),
        [(devices, LANES), shape] + send_shapes(1),
        (fine, vectors, inverse, diagonal_block, coupling, prolongator, aggregate, *around[-1]),
        rows,
    )
    parts.append(further)
    around.append(exchange(sends))
    gathered = lax.all_to_all(payload.reshape(devices, 1, LANES), ("sx", "sy"), 0, 0).reshape(devices, LANES)
    correction, field = call(
        finish_kernel,
        [(3, 1, LANES), shape],
        (gathered, vectors, source, inverse, diagonal_block, coupling, *parts) + tuple(h for halo in around for h in halo),
    )
    return field, correction.reshape(3, 1, 1, NA)


def solution(mesh):
    in_specs = (
        P(None, "sx", "sy", None),
        P(None, "sx", "sy", None),
        P(None, None, None, "sx", "sy", None),
        P(None, None, "sx", "sy", None),
        P(None, None, "sx", "sy", None),
        P("sx", "sy", None),
    )
    out_specs = (P(None, "sx", "sy", None), P(None, "sx", "sy", None))
    return jax.shard_map(local, mesh=mesh, in_specs=in_specs, out_specs=out_specs, check_vma=False)
```

```python
import functools

import jax
import jax.numpy as jnp
from jax import lax
from jax.experimental import pallas as pl
from jax.experimental.pallas import tpu as pltpu
from jax.sharding import PartitionSpec as P

NU = 2
KC = 4
NA = 128
LANES = 128

damping = 0.8
R3 = range(3)
VMEM = pltpu.VMEM
f32 = jnp.float32
bf16 = jnp.bfloat16

PAIRS = [(i, i + lag) for lag in range(KC + 1) for i in range(KC) if i + lag <= KC]
LAG_START = [min(p for p, (i, j) in enumerate(PAIRS) if j - i == lag) for lag in range(KC + 1)]
LAG_COUNT = [sum(1 for i, j in PAIRS if j - i == lag) for lag in range(KC + 1)]


def pair_exchange(x, axis, odd):
    n = lax.axis_size(axis)
    if odd:
        pairs = [(k, (k + 1) % n) for k in range(1, n, 2)] + [((k + 1) % n, k) for k in range(1, n, 2)]
    else:
        pairs = [(k, k ^ 1) for k in range(n)]
    return lax.ppermute(x, axis, pairs)


def exchange(sends):
    yb, xb, ya, xa = sends
    return (
        pair_exchange(yb, "sy", True),
        pair_exchange(xb, "sx", True),
        pair_exchange(ya, "sy", False),
        pair_exchange(xa, "sx", False),
    )


def iota(shape, dim):
    return lax.broadcasted_iota(jnp.int32, shape, dim)


def sides(axis):
    index = lax.axis_index(axis)
    return index % 2 == 0, index == 0, index == lax.axis_size(axis) - 1


def load_field(ref):
    return [[ref[c, x] for x in range(ref.shape[1])] for c in R3]


def store_field(ref, field):
    for c in R3:
        for x in range(ref.shape[1]):
            ref[c, x] = field[c][x]


def times(block, vector):
    return [block(i, 0) * vector[0] + block(i, 1) * vector[1] + block(i, 2) * vector[2] for i in R3]


def transposed_times(block, vector):
    return [block(0, i) * vector[0] + block(1, i) * vector[1] + block(2, i) * vector[2] for i in R3]


def send_faces(fields, coupling, sends):
    yb, xb, ya, xa = sends
    nx = len(fields[0][0])
    ny = fields[0][0][0].shape[0]
    even_x, _, _ = sides("sx")
    even_y, _, _ = sides("sy")
    for number, field in enumerate(fields):
        for x in range(nx):
            top = transposed_times(
                lambda i, j: coupling[1, i, j, x, ny - 1 : ny], [field[j][x][ny - 1 : ny] for j in R3]
            )
            for i in R3:
                bottom = field[i][x][0:1]
                row = (3 * number + i) * nx + x
                ya[row : row + 1] = jnp.where(even_y, top[i], bottom)
                yb[row : row + 1] = jnp.where(even_y, bottom, top[i])
        top = transposed_times(lambda i, j: coupling[0, i, j, nx - 1], [field[j][nx - 1] for j in R3])
        for i in R3:
            bottom = field[i][0]
            xa[3 * number + i] = jnp.where(even_x, top[i], bottom)
            xb[3 * number + i] = jnp.where(even_x, bottom, top[i])


def halos(received, nx):
    xa, xb, ya, yb = received
    even_x, first_x, last_x = sides("sx")
    even_y, first_y, last_y = sides("sy")
    up_x = [jnp.where(last_x, 0.0, jnp.where(even_x, xa[i], xb[i])) for i in R3]
    low_x = [jnp.where(first_x, 0.0, jnp.where(even_x, xb[i], xa[i])) for i in R3]
    up_y = jnp.where(last_y, 0.0, jnp.where(even_y, ya, yb))
    low_y = jnp.where(first_y, 0.0, jnp.where(even_y, yb, ya))
    up_y = [[up_y[i * nx + x : i * nx + x + 1] for x in range(nx)] for i in R3]
    low_y = [[low_y[i * nx + x : i * nx + x + 1] for x in range(nx)] for i in R3]
    return up_x, low_x, up_y, low_y


def read_halos(refs, nx, number=0):
    yb, xb, ya, xa = refs
    at = 3 * number
    rows = slice(at * nx, (at + 3) * nx)
    return [xa[at + i] for i in R3], [xb[at + i] for i in R3], ya[rows], yb[rows]


def apply_operator(field, around, diagonal, coupling):
    up_x, low_x, up_y, low_y = around
    nx = len(field[0])
    ny, nz = field[0][0].shape
    row = iota((ny, nz), 0)
    lane = iota((ny, nz), 1)
    result = [[None] * nx for _ in R3]
    for x in range(nx):
        own = [field[j][x] for j in R3]
        total = times(lambda i, j: diagonal[i, j, x], own)
        upper = [field[j][x + 1] if x + 1 < nx else up_x[j] for j in R3]
        part = times(lambda i, j: coupling[0, i, j, x], upper)
        total = [total[i] + part[i] for i in R3]
        if x:
            part = transposed_times(lambda i, j: coupling[0, i, j, x - 1], [field[j][x - 1] for j in R3])
        else:
            part = low_x
        total = [total[i] + part[i] for i in R3]
        upper = [jnp.where(row == ny - 1, up_y[j][x], pltpu.roll(own[j], ny - 1, 0)) for j in R3]
        part = times(lambda i, j: coupling[1, i, j, x], upper)
        total = [total[i] + part[i] for i in R3]
        part = transposed_times(lambda i, j: coupling[1, i, j, x], own)
        total = [total[i] + jnp.where(row == 0, low_y[i][x], pltpu.roll(part[i], 1, 0)) for i in R3]
        upper = [jnp.where(lane == nz - 1, 0.0, pltpu.roll(own[j], nz - 1, 1)) for j in R3]
        part = times(lambda i, j: coupling[2, i, j, x], upper)
        total = [total[i] + part[i] for i in R3]
        part = transposed_times(lambda i, j: coupling[2, i, j, x], own)
        total = [total[i] + jnp.where(lane == 0, 0.0, pltpu.roll(part[i], 1, 1)) for i in R3]
        for i in R3:
            result[i][x] = total[i]
    return result


def inverse_of(diagonal, x):
    m = [[diagonal[i, j, x] for j in R3] for i in R3]
    adjugate = [
        [
            m[(j + 1) % 3][(i + 1) % 3] * m[(j + 2) % 3][(i + 2) % 3]
            - m[(j + 1) % 3][(i + 2) % 3] * m[(j + 2) % 3][(i + 1) % 3]
            for j in R3
        ]
        for i in R3
    ]
    determinant = m[0][0] * adjugate[0][0] + m[0][1] * adjugate[1][0] + m[0][2] * adjugate[2][0]
    return [[adjugate[i][j] / determinant for j in R3] for i in R3]


def relaxed(field, defect, inverse):
    result = [[None] * len(field[0]) for _ in R3]
    for x in range(len(field[0])):
        change = times(lambda i, j: inverse[i, j, x], [defect[i][x] for i in R3])
        for i in R3:
            result[i][x] = field[i][x] + damping * change[i]
    return result


def defect_of(source, image):
    return [[source[i, x] - image[i][x] for x in range(len(image[0]))] for i in R3]


def negated(image):
    return [[-value for value in row] for row in image]


def restrict(field, prolongator, members, rows):
    nx = len(field[0])
    ny, nz = field[0][0].shape
    for x in range(nx):
        values = transposed_times(lambda i, j: prolongator[i, j, x], [field[j][x] for j in R3])
        for k in R3:
            high = values[k].astype(bf16).astype(f32)
            rest = values[k] - high
            middle = rest.astype(bf16).astype(f32)
            low = rest - middle
            for part, value in enumerate((high, middle, low)):
                rows[pl.ds(x * ny * 16 + 3 * part + k, ny, stride=16), :] = value
    left = [rows[block * 16 : block * 16 + 16, :].astype(bf16) for block in range(nx * ny)]
    total = lax.dot_general(
        jnp.concatenate(left, axis=1), members[...], (((1,), (0,)), ((), ())), preferred_element_type=f32
    )
    return [total[k : k + 1] + (total[3 + k : 4 + k] + total[6 + k : 7 + k]) for k in R3]


def prolong(coarse, prolongator, aggregate):
    nx, ny, nz = aggregate.shape
    tables = [jnp.broadcast_to(coarse[k], (ny, nz)) for k in R3]
    result = [[None] * nx for _ in R3]
    for x in range(nx):
        ids = aggregate[x]
        picked = [jnp.take_along_axis(tables[k], ids, axis=1, mode="promise_in_bounds") for k in R3]
        value = times(lambda i, j: prolongator[i, j, x], picked)
        for i in R3:
            result[i][x] = value[i]
    return result


def two_sum(a, b):
    s = a + b
    t = s - a
    return s, (a - (s - t)) + (b - t)


def quick_sum(a, b):
    s = a + b
    return s, b - (s - a)


def halves(a):
    c = 4097.0 * a
    high = c - (c - a)
    return high, a - high


def two_product(a, b):
    p = a * b
    ah, al = halves(a)
    bh, bl = halves(b)
    return p, ((ah * bh - p) + ah * bl + al * bh) + al * bl


def dd_add(x, y):
    s, e = two_sum(x[0], y[0])
    return quick_sum(s, e + (x[1] + y[1]))


def dd_neg(x):
    return -x[0], -x[1]


def dd_mul(x, y):
    p, e = two_product(x[0], y[0])
    return p, e + (x[0] * y[1] + x[1] * y[0])


def dd_div(x, y, inverse):
    first = x[0] * inverse
    p, e = two_product(first, y[0])
    rest = ((x[0] - p) - e) + (x[1] - first * y[1])
    return quick_sum(first, rest * inverse)


def plain_total(terms):
    while len(terms) > 1:
        terms = [terms[k] + terms[k + 1] if k + 1 < len(terms) else terms[k] for k in range(0, len(terms), 2)]
    return terms[0]


def dd_total(terms):
    highs, lows = [t[0] for t in terms], [plain_total([t[1] for t in terms])]
    while len(highs) > 1:
        pairs = [two_sum(highs[k], highs[k + 1]) for k in range(0, len(highs) - 1, 2)]
        lows += [e for _, e in pairs]
        highs = [s for s, _ in pairs] + highs[2 * len(pairs) :]
    return quick_sum(highs[0], plain_total(lows))


def limbs(total):
    first = (total[0] + 1536.0) - 1536.0
    rest = total[0] - first
    second = (rest + 1.5 * 2.0**-7) - 1.5 * 2.0**-7
    return first, second, (rest - second) + total[1]


def power_of_two(x):
    scale = jnp.full_like(x, 2.0**-126)
    inverse = jnp.full_like(x, 2.0**126)
    for step in (64, 64, 64, 32, 16, 8, 4, 2, 1):
        larger = scale * 2.0**step
        take = (x >= larger) & (larger <= 2.0**126)
        scale = jnp.where(take, larger, scale)
        inverse = jnp.where(take, inverse * 2.0**-step, inverse)
    return scale, inverse


def members_kernel(aggregate, members):
    nx, ny, nz = aggregate.shape
    which = iota((nz, NA), 1)
    for x in range(nx):
        ids = jnp.transpose(aggregate[x].astype(f32)).astype(jnp.int32)
        for y in range(ny):
            own = jnp.broadcast_to(ids[:, y : y + 1], (nz, NA))
            at = (x * ny + y) * nz
            members[at : at + nz, :] = jnp.where(own == which, 1.0, 0.0).astype(bf16)


def inverse_kernel(diagonal, inverse):
    for x in range(diagonal.shape[2]):
        block = inverse_of(diagonal, x)
        for i in R3:
            for j in R3:
                inverse[i, j, x] = block[i][j]


def faces_kernel(field, coupling, *sends):
    send_faces([load_field(field)], coupling, sends)


def sweep_kernel(field, source, inverse, diagonal, coupling, *refs):
    received, new_field, sends = refs[:4], refs[4], refs[5:]
    own = load_field(field)
    nx = len(own[0])
    image = apply_operator(own, halos(read_halos(received, nx), nx), diagonal, coupling)
    new = relaxed(own, defect_of(source, image), inverse)
    store_field(new_field, new)
    send_faces([new], coupling, sends)


def residual_kernel(field, source, inverse, diagonal, coupling, prolongator, aggregate, members, *refs):
    received, (vectors, fine, further), sends, rows = refs[:4], refs[4:7], refs[7:11], refs[11]
    own = load_field(field)
    nx = len(own[0])
    image = apply_operator(own, halos(read_halos(received, nx), nx), diagonal, coupling)
    defect = defect_of(source, image)
    coarse = restrict(defect, prolongator, members, rows)
    row = iota((8, LANES), 0)
    for k in R3:
        vectors[k] = jnp.where(row == 0, coarse[k], 0.0)
    new = prolong(coarse, prolongator, aggregate)
    store_field(fine, new)
    swept = relaxed(own, defect, inverse)
    store_field(further, swept)
    send_faces([new, swept], coupling, sends)


def krylov_kernel(step, fine_in, vectors_in, inverse, diagonal, coupling, prolongator, aggregate, members, *refs):
    received, (vectors, fine, further), sends, rows = refs[:4], refs[4:7], refs[7:11], refs[11]
    own = load_field(fine_in)
    nx = len(own[0])
    image = apply_operator(own, halos(read_halos(received, nx), nx), diagonal, coupling)
    coarse = restrict(image, prolongator, members, rows)
    row = iota((8, LANES), 0)
    for k in R3:
        vectors[k] = jnp.where(row == step, coarse[k], vectors_in[k])
    new = prolong(coarse, prolongator, aggregate)
    store_field(fine, new)
    swept = relaxed(own, negated(image), inverse)
    store_field(further, swept)
    send_faces([new, swept], coupling, sends)


def gram_kernel(step, fine_in, vectors_in, inverse, diagonal, coupling, prolongator, aggregate, members, *refs):
    received, payload, further, sends, rows = refs[:4], refs[4], refs[5], refs[6:10], refs[10]
    own = load_field(fine_in)
    nx = len(own[0])
    image = apply_operator(own, halos(read_halos(received, nx), nx), diagonal, coupling)
    swept = relaxed(own, negated(image), inverse)
    store_field(further, swept)
    send_faces([swept], coupling, sends)
    coarse = restrict(image, prolongator, members, rows)
    shape = (8, LANES)
    row, lane = iota(shape, 0), iota(shape, 1)
    all_vectors = [jnp.where(row == step, coarse[k], vectors_in[k]) for k in R3]
    largest = jnp.maximum(jnp.maximum(jnp.abs(all_vectors[0]), jnp.abs(all_vectors[1])), jnp.abs(all_vectors[2]))
    largest = jnp.broadcast_to(jnp.max(largest, axis=1, keepdims=True), shape)
    scale, inverse = power_of_two(largest)
    unit = [all_vectors[k] * inverse for k in R3]
    out = jnp.zeros(shape, f32)
    for lag in range(KC + 1):
        other = [pltpu.roll(u, 8 - lag, 0) if lag else u for u in unit]
        total = dd_total([two_product(unit[k], other[k]) for k in R3])
        sums = [jnp.broadcast_to(jnp.sum(part, axis=1, keepdims=True), shape) for part in limbs(total)]
        total = two_sum(sums[0], sums[1])
        total = quick_sum(total[0], total[1] + sums[2])
        scale_j, inverse_j = (pltpu.roll(s, 8 - lag, 0) if lag else s for s in (scale, inverse))
        pair = row + LAG_START[lag]
        here = row < LAG_COUNT[lag]
        for slot, value in enumerate((*total, scale, scale, scale_j, scale_j, inverse, inverse_j)):
            out = jnp.where(here & (lane == pair + 16 * slot), value, out)
    line = jnp.sum(out, axis=0, keepdims=True)
    payload[...] = jnp.broadcast_to(line, payload.shape)


def combine(gathered):
    n = gathered.shape[0]
    inverse = jnp.min(gathered[...], axis=0, keepdims=True)
    inverse_i = pltpu.roll(jnp.broadcast_to(inverse, (8, LANES)), 32, 1)
    inverse_j = pltpu.roll(jnp.broadcast_to(inverse, (8, LANES)), 16, 1)
    lane = iota((8, LANES), 1)
    inv_i = jnp.where(lane < 16, inverse_i, pltpu.roll(inverse_i, 16, 1))
    inv_j = jnp.where(lane < 16, inverse_j, pltpu.roll(inverse_j, 16, 1))
    terms = []
    for start in range(0, n, 8):
        block = gathered[start : start + 8, :]
        weight = (pltpu.roll(block, LANES - 32, 1) * inv_i) * (pltpu.roll(block, LANES - 64, 1) * inv_j)
        terms.append((jnp.where(lane < 32, block * weight, 0.0), jnp.zeros((8, LANES), f32)))
    total = dd_total(terms)
    for by in (4, 2, 1):
        total = dd_add(total, tuple(pltpu.roll(t, by, 0) for t in total))
    total = dd_add(total, (pltpu.roll(total[0], LANES - 16, 1), jnp.zeros((8, LANES), f32)))

    def spread(value, at):
        return jnp.broadcast_to(value[:, at : at + 1], (8, LANES))

    gram = {}
    for p, (i, j) in enumerate(PAIRS):
        gram[i, j] = gram[j, i] = (spread(total[0], p), spread(total[1], p))
    at_i = {i: p for p, (i, j) in enumerate(PAIRS) if j == i}
    unscale = [spread(inverse_i, at_i[i]) for i in range(KC)] + [spread(inverse_j, PAIRS.index((0, KC)))]
    scale0 = power_of_two(1.25 / unscale[0])[0]
    growth = [power_of_two(1.25 * unscale[j] / unscale[j + 1])[0] for j in range(KC)]
    zero = jnp.zeros((8, LANES), f32)
    one = jnp.ones((8, LANES), f32)
    residual = [(one, zero)]
    direction = [(one, zero)]
    answer = []
    rr = gram[0, 0]
    start = rr[0]
    inverse_rr = 1.0 / rr[0]
    for it in range(KC):
        image = [None] + [(growth[j] * d[0], growth[j] * d[1]) for j, d in enumerate(direction)]
        last = it + 1 == KC
        rows = [
            dd_total([dd_mul(gram[i, j], image[j]) for j in range(1, it + 2)]) for i in range(it + 1 if last else it + 2)
        ]
        curvature = dd_total([dd_mul(direction[i], rows[i]) for i in range(it + 1)])
        live = rr[0] > 1e-12 * start
        curvature = tuple(jnp.where(live, c, o) for c, o in zip(curvature, (one, zero)))
        alpha = dd_div(rr, curvature, 1.0 / curvature[0])
        alpha = tuple(jnp.where(live, a, 0.0) for a in alpha)
        steps = [dd_mul(alpha, d) for d in direction]
        answer = [dd_add(a, s) for a, s in zip(answer, steps)] + steps[len(answer) :]
        if last:
            break
        square = dd_total([dd_mul(image[i], rows[i]) for i in range(1, it + 2)])
        new = dd_add(dd_mul(quick_sum(*dd_mul(alpha, alpha)), square), dd_neg(rr))
        new = tuple(jnp.where(live, n, 0.0) for n in new)
        moved = [None] + [dd_neg(dd_mul(alpha, image[j])) for j in range(1, it + 2)]
        residual = [residual[0]] + [
            dd_add(residual[j], moved[j]) if j < len(residual) else quick_sum(*moved[j]) for j in range(1, it + 2)
        ]
        beta = dd_div(new, rr, inverse_rr)
        direction = [dd_add(residual[j], dd_mul(beta, direction[j])) for j in range(it + 1)] + residual[it + 1 :]
        rr = new
        inverse_rr = 1.0 / jnp.where(rr[0] > 0.0, rr[0], 1.0)
    return [a[0] * (scale0 * unscale[j]) for j, a in enumerate(answer)]


def finish_kernel(gathered, vectors, source, inverse, diagonal, coupling, *refs):
    parts, refs = refs[: KC + 1], refs[KC + 1 :]
    received, (correction, new_field) = refs[: 4 * (KC + 1)], refs[4 * (KC + 1) :]
    weights = combine(gathered)
    for k in R3:
        total = None
        for j in range(KC):
            part = weights[j][0:1] * vectors[k, j : j + 1, :]
            total = part if total is None else total + part
        correction[k] = total
    own = load_field(parts[0])
    nx = len(own[0])
    around = read_halos(received[:4], nx, 1)
    for j in range(KC):
        weight = weights[j]
        own = [[own[c][x] + weight * parts[j + 1][c, x] for x in range(nx)] for c in R3]
        part = read_halos(received[4 * (j + 1) : 4 * (j + 2)], nx, 1 if j + 1 < KC else 0)
        around = (
            [a + weight * b for a, b in zip(around[0], part[0])],
            [a + weight * b for a, b in zip(around[1], part[1])],
            around[2] + weight[0:1] * part[2],
            around[3] + weight[0:1] * part[3],
        )
    image = apply_operator(own, halos(around, nx), diagonal, coupling)
    store_field(new_field, relaxed(own, defect_of(source, image), inverse))


def call(kernel, out_shapes, inputs, scratch=(), dtype=f32):
    return pl.pallas_call(
        kernel,
        out_shape=[jax.ShapeDtypeStruct(s, dtype) for s in out_shapes],
        in_specs=[pl.BlockSpec(memory_space=VMEM)] * len(inputs),
        out_specs=[pl.BlockSpec(memory_space=VMEM)] * len(out_shapes),
        scratch_shapes=list(scratch),
        compiler_params=pltpu.CompilerParams(vmem_limit_bytes=16 * 2**20),
    )(*inputs)


def local(source, initial_guess, coupling, diagonal_block, prolongator, aggregate):
    _, nx, ny, nz = source.shape
    devices = lax.axis_size("sx") * lax.axis_size("sy")
    shape = source.shape
    vector_shape = (3, 8, LANES)
    rows = [pltpu.VMEM((nx * ny * 16, nz), f32)]

    def send_shapes(fields):
        faces, lines = (3 * fields, ny, nz), (3 * fields * ny, nz)
        return [lines, faces, lines, faces]

    received = exchange(call(faces_kernel, send_shapes(1), (initial_guess, coupling)))
    (inverse,) = call(inverse_kernel, [diagonal_block.shape], (diagonal_block,))
    (members,) = call(members_kernel, [(nx * ny * nz, NA)], (aggregate,), dtype=bf16)
    field = initial_guess
    for _ in range(NU):
        field, *sends = call(
            sweep_kernel, [shape] + send_shapes(1), (field, source, inverse, diagonal_block, coupling, *received)
        )
        received = exchange(sends)
    vectors, fine, further, *sends = call(
        residual_kernel,
        [vector_shape, shape, shape] + send_shapes(2),
        (field, source, inverse, diagonal_block, coupling, prolongator, aggregate, members, *received),
        rows,
    )
    parts, around = [further], [exchange(sends)]
    for step in range(1, KC):
        vectors, fine, further, *sends = call(
            functools.partial(krylov_kernel, step),
            [vector_shape, shape, shape] + send_shapes(2),
            (fine, vectors, inverse, diagonal_block, coupling, prolongator, aggregate, members, *around[-1]),
            rows,
        )
        parts.append(further)
        around.append(exchange(sends))
    payload, further, *sends = call(
        functools.partial(gram_kernel, KC),
        [(devices, LANES), shape] + send_shapes(1),
        (fine, vectors, inverse, diagonal_block, coupling, prolongator, aggregate, members, *around[-1]),
        rows,
    )
    parts.append(further)
    around.append(exchange(sends))
    gathered = lax.all_to_all(payload.reshape(devices, 1, LANES), ("sx", "sy"), 0, 0).reshape(devices, LANES)
    correction, field = call(
        finish_kernel,
        [(3, 1, LANES), shape],
        (gathered, vectors, source, inverse, diagonal_block, coupling, *parts) + tuple(h for halo in around for h in halo),
    )
    return field, correction.reshape(3, 1, 1, NA)


def solution(mesh):
    in_specs = (
        P(None, "sx", "sy", None),
        P(None, "sx", "sy", None),
        P(None, None, None, "sx", "sy", None),
        P(None, None, "sx", "sy", None),
        P(None, None, "sx", "sy", None),
        P("sx", "sy", None),
    )
    out_specs = (P(None, "sx", "sy", None), P(None, "sx", "sy", None))
    return jax.shard_map(local, mesh=mesh, in_specs=in_specs, out_specs=out_specs, check_vma=False)
```

```python
import functools

import jax
import jax.numpy as jnp
from jax import lax
from jax.experimental import pallas as pl
from jax.experimental.pallas import tpu as pltpu
from jax.sharding import PartitionSpec as P

NU = 2
KC = 4
NA = 128
LANES = 128

damping = 0.8
R3 = range(3)
VMEM = pltpu.VMEM
f32 = jnp.float32
bf16 = jnp.bfloat16

PAIRS = [(i, i + lag) for lag in range(KC + 1) for i in range(KC) if i + lag <= KC]
LAG_START = [min(p for p, (i, j) in enumerate(PAIRS) if j - i == lag) for lag in range(KC + 1)]
LAG_COUNT = [sum(1 for i, j in PAIRS if j - i == lag) for lag in range(KC + 1)]


def pair_exchange(x, axis, odd):
    n = lax.axis_size(axis)
    if odd:
        pairs = [(k, (k + 1) % n) for k in range(1, n, 2)] + [((k + 1) % n, k) for k in range(1, n, 2)]
    else:
        pairs = [(k, k ^ 1) for k in range(n)]
    return lax.ppermute(x, axis, pairs)


def exchange(sends):
    yb, xb, ya, xa = sends
    return (
        pair_exchange(yb, "sy", True),
        pair_exchange(xb, "sx", True),
        pair_exchange(ya, "sy", False),
        pair_exchange(xa, "sx", False),
    )


def iota(shape, dim):
    return lax.broadcasted_iota(jnp.int32, shape, dim)


def sides(axis):
    index = lax.axis_index(axis)
    return index % 2 == 0, index == 0, index == lax.axis_size(axis) - 1


def load_field(ref):
    return [[ref[c, x] for x in range(ref.shape[1])] for c in R3]


def store_field(ref, field):
    for c in R3:
        for x in range(ref.shape[1]):
            ref[c, x] = field[c][x]


def times(block, vector):
    return [block(i, 0) * vector[0] + block(i, 1) * vector[1] + block(i, 2) * vector[2] for i in R3]


def transposed_times(block, vector):
    return [block(0, i) * vector[0] + block(1, i) * vector[1] + block(2, i) * vector[2] for i in R3]


def send_faces(fields, coupling, sends):
    yb, xb, ya, xa = sends
    nx = len(fields[0][0])
    ny = fields[0][0][0].shape[0]
    even_x, _, _ = sides("sx")
    even_y, _, _ = sides("sy")
    for number, field in enumerate(fields):
        for x in range(nx):
            top = transposed_times(
                lambda i, j: coupling[1, i, j, x, ny - 1 : ny], [field[j][x][ny - 1 : ny] for j in R3]
            )
            for i in R3:
                bottom = field[i][x][0:1]
                row = (3 * number + i) * nx + x
                ya[row : row + 1] = jnp.where(even_y, top[i], bottom)
                yb[row : row + 1] = jnp.where(even_y, bottom, top[i])
        top = transposed_times(lambda i, j: coupling[0, i, j, nx - 1], [field[j][nx - 1] for j in R3])
        for i in R3:
            bottom = field[i][0]
            xa[3 * number + i] = jnp.where(even_x, top[i], bottom)
            xb[3 * number + i] = jnp.where(even_x, bottom, top[i])


def halos(received, nx):
    xa, xb, ya, yb = received
    even_x, first_x, last_x = sides("sx")
    even_y, first_y, last_y = sides("sy")
    up_x = [jnp.where(last_x, 0.0, jnp.where(even_x, xa[i], xb[i])) for i in R3]
    low_x = [jnp.where(first_x, 0.0, jnp.where(even_x, xb[i], xa[i])) for i in R3]
    up_y = jnp.where(last_y, 0.0, jnp.where(even_y, ya, yb))
    low_y = jnp.where(first_y, 0.0, jnp.where(even_y, yb, ya))
    up_y = [[up_y[i * nx + x : i * nx + x + 1] for x in range(nx)] for i in R3]
    low_y = [[low_y[i * nx + x : i * nx + x + 1] for x in range(nx)] for i in R3]
    return up_x, low_x, up_y, low_y


def read_halos(refs, nx, number=0):
    yb, xb, ya, xa = refs
    at = 3 * number
    rows = slice(at * nx, (at + 3) * nx)
    return [xa[at + i] for i in R3], [xb[at + i] for i in R3], ya[rows], yb[rows]


def apply_operator(field, around, diagonal, coupling):
    up_x, low_x, up_y, low_y = around
    nx = len(field[0])
    ny, nz = field[0][0].shape
    row = iota((ny, nz), 0)
    lane = iota((ny, nz), 1)
    result = [[None] * nx for _ in R3]
    for x in range(nx):
        own = [field[j][x] for j in R3]
        total = times(lambda i, j: diagonal[i, j, x], own)
        upper = [field[j][x + 1] if x + 1 < nx else up_x[j] for j in R3]
        part = times(lambda i, j: coupling[0, i, j, x], upper)
        total = [total[i] + part[i] for i in R3]
        if x:
            part = transposed_times(lambda i, j: coupling[0, i, j, x - 1], [field[j][x - 1] for j in R3])
        else:
            part = low_x
        total = [total[i] + part[i] for i in R3]
        upper = [jnp.where(row == ny - 1, up_y[j][x], pltpu.roll(own[j], ny - 1, 0)) for j in R3]
        part = times(lambda i, j: coupling[1, i, j, x], upper)
        total = [total[i] + part[i] for i in R3]
        part = transposed_times(lambda i, j: coupling[1, i, j, x], own)
        total = [total[i] + jnp.where(row == 0, low_y[i][x], pltpu.roll(part[i], 1, 0)) for i in R3]
        upper = [jnp.where(lane == nz - 1, 0.0, pltpu.roll(own[j], nz - 1, 1)) for j in R3]
        part = times(lambda i, j: coupling[2, i, j, x], upper)
        total = [total[i] + part[i] for i in R3]
        part = transposed_times(lambda i, j: coupling[2, i, j, x], own)
        total = [total[i] + jnp.where(lane == 0, 0.0, pltpu.roll(part[i], 1, 1)) for i in R3]
        for i in R3:
            result[i][x] = total[i]
    return result


def inverse_of(diagonal, x):
    m = [[diagonal[i, j, x] for j in R3] for i in R3]
    adjugate = [
        [
            m[(j + 1) % 3][(i + 1) % 3] * m[(j + 2) % 3][(i + 2) % 3]
            - m[(j + 1) % 3][(i + 2) % 3] * m[(j + 2) % 3][(i + 1) % 3]
            for j in R3
        ]
        for i in R3
    ]
    determinant = m[0][0] * adjugate[0][0] + m[0][1] * adjugate[1][0] + m[0][2] * adjugate[2][0]
    return [[adjugate[i][j] / determinant for j in R3] for i in R3]


def relaxed(field, defect, inverse):
    result = [[None] * len(field[0]) for _ in R3]
    for x in range(len(field[0])):
        change = times(lambda i, j: inverse[i, j, x], [defect[i][x] for i in R3])
        for i in R3:
            result[i][x] = field[i][x] + damping * change[i]
    return result


def defect_of(source, image):
    return [[source[i, x] - image[i][x] for x in range(len(image[0]))] for i in R3]


def negated(image):
    return [[-value for value in row] for row in image]


def restrict(field, prolongator, members, rows):
    nx = len(field[0])
    ny, nz = field[0][0].shape
    for x in range(nx):
        values = transposed_times(lambda i, j: prolongator[i, j, x], [field[j][x] for j in R3])
        for k in R3:
            high = values[k].astype(bf16).astype(f32)
            rest = values[k] - high
            middle = rest.astype(bf16).astype(f32)
            low = rest - middle
            for part, value in enumerate((high, middle, low)):
                rows[pl.ds(x * ny * 24 + 3 * part + k, ny, stride=24), :] = value
    left = [rows[block * 24 : block * 24 + 16, :].astype(bf16) for block in range(nx * ny)]
    total = lax.dot_general(
        jnp.concatenate(left, axis=1), members[...], (((1,), (0,)), ((), ())), preferred_element_type=f32
    )
    return [total[k : k + 1] + (total[3 + k : 4 + k] + total[6 + k : 7 + k]) for k in R3]


def prolong(coarse, prolongator, aggregate):
    nx, ny, nz = aggregate.shape
    tables = [jnp.broadcast_to(coarse[k], (ny, nz)) for k in R3]
    result = [[None] * nx for _ in R3]
    for x in range(nx):
        ids = aggregate[x]
        picked = [jnp.take_along_axis(tables[k], ids, axis=1, mode="promise_in_bounds") for k in R3]
        value = times(lambda i, j: prolongator[i, j, x], picked)
        for i in R3:
            result[i][x] = value[i]
    return result


def two_sum(a, b):
    s = a + b
    t = s - a
    return s, (a - (s - t)) + (b - t)


def quick_sum(a, b):
    s = a + b
    return s, b - (s - a)


def halves(a):
    c = 4097.0 * a
    high = c - (c - a)
    return high, a - high


def two_product(a, b):
    p = a * b
    ah, al = halves(a)
    bh, bl = halves(b)
    return p, ((ah * bh - p) + ah * bl + al * bh) + al * bl


def dd_add(x, y):
    s, e = two_sum(x[0], y[0])
    return quick_sum(s, e + (x[1] + y[1]))


def dd_neg(x):
    return -x[0], -x[1]


def dd_mul(x, y):
    p, e = two_product(x[0], y[0])
    return p, e + (x[0] * y[1] + x[1] * y[0])


def dd_div(x, y, inverse):
    first = x[0] * inverse
    p, e = two_product(first, y[0])
    rest = ((x[0] - p) - e) + (x[1] - first * y[1])
    return quick_sum(first, rest * inverse)


def plain_total(terms):
    while len(terms) > 1:
        terms = [terms[k] + terms[k + 1] if k + 1 < len(terms) else terms[k] for k in range(0, len(terms), 2)]
    return terms[0]


def dd_total(terms):
    highs, lows = [t[0] for t in terms], [plain_total([t[1] for t in terms])]
    while len(highs) > 1:
        pairs = [two_sum(highs[k], highs[k + 1]) for k in range(0, len(highs) - 1, 2)]
        lows += [e for _, e in pairs]
        highs = [s for s, _ in pairs] + highs[2 * len(pairs) :]
    return quick_sum(highs[0], plain_total(lows))


def limbs(total):
    first = (total[0] + 1536.0) - 1536.0
    rest = total[0] - first
    second = (rest + 1.5 * 2.0**-7) - 1.5 * 2.0**-7
    return first, second, (rest - second) + total[1]


def power_of_two(x):
    scale = jnp.full_like(x, 2.0**-126)
    inverse = jnp.full_like(x, 2.0**126)
    for step in (64, 64, 64, 32, 16, 8, 4, 2, 1):
        larger = scale * 2.0**step
        take = (x >= larger) & (larger <= 2.0**126)
        scale = jnp.where(take, larger, scale)
        inverse = jnp.where(take, inverse * 2.0**-step, inverse)
    return scale, inverse


def members_kernel(aggregate, members):
    nx, ny, nz = aggregate.shape
    which = iota((nz, NA), 1)
    for x in range(nx):
        ids = jnp.transpose(aggregate[x].astype(f32)).astype(jnp.int32)
        for y in range(ny):
            own = jnp.broadcast_to(ids[:, y : y + 1], (nz, NA))
            at = (x * ny + y) * nz
            members[at : at + nz, :] = jnp.where(own == which, 1.0, 0.0).astype(bf16)


def inverse_kernel(diagonal, inverse):
    for x in range(diagonal.shape[2]):
        block = inverse_of(diagonal, x)
        for i in R3:
            for j in R3:
                inverse[i, j, x] = block[i][j]


def faces_kernel(field, coupling, *sends):
    send_faces([load_field(field)], coupling, sends)


def sweep_kernel(field, source, inverse, diagonal, coupling, *refs):
    received, new_field, sends = refs[:4], refs[4], refs[5:]
    own = load_field(field)
    nx = len(own[0])
    image = apply_operator(own, halos(read_halos(received, nx), nx), diagonal, coupling)
    new = relaxed(own, defect_of(source, image), inverse)
    store_field(new_field, new)
    send_faces([new], coupling, sends)


def residual_kernel(field, source, inverse, diagonal, coupling, prolongator, aggregate, members, *refs):
    received, (vectors, fine, further), sends, rows = refs[:4], refs[4:7], refs[7:11], refs[11]
    own = load_field(field)
    nx = len(own[0])
    image = apply_operator(own, halos(read_halos(received, nx), nx), diagonal, coupling)
    defect = defect_of(source, image)
    coarse = restrict(defect, prolongator, members, rows)
    row = iota((8, LANES), 0)
    for k in R3:
        vectors[k] = jnp.where(row == 0, coarse[k], 0.0)
    new = prolong(coarse, prolongator, aggregate)
    store_field(fine, new)
    swept = relaxed(own, defect, inverse)
    store_field(further, swept)
    send_faces([new, swept], coupling, sends)


def krylov_kernel(step, fine_in, vectors_in, inverse, diagonal, coupling, prolongator, aggregate, members, *refs):
    received, (vectors, fine, further), sends, rows = refs[:4], refs[4:7], refs[7:11], refs[11]
    own = load_field(fine_in)
    nx = len(own[0])
    image = apply_operator(own, halos(read_halos(received, nx), nx), diagonal, coupling)
    coarse = restrict(image, prolongator, members, rows)
    row = iota((8, LANES), 0)
    for k in R3:
        vectors[k] = jnp.where(row == step, coarse[k], vectors_in[k])
    new = prolong(coarse, prolongator, aggregate)
    store_field(fine, new)
    swept = relaxed(own, negated(image), inverse)
    store_field(further, swept)
    send_faces([new, swept], coupling, sends)


def gram_kernel(step, fine_in, vectors_in, inverse, diagonal, coupling, prolongator, aggregate, members, *refs):
    received, payload, further, sends, rows = refs[:4], refs[4], refs[5], refs[6:10], refs[10]
    own = load_field(fine_in)
    nx = len(own[0])
    image = apply_operator(own, halos(read_halos(received, nx), nx), diagonal, coupling)
    swept = relaxed(own, negated(image), inverse)
    store_field(further, swept)
    send_faces([swept], coupling, sends)
    coarse = restrict(image, prolongator, members, rows)
    shape = (8, LANES)
    row, lane = iota(shape, 0), iota(shape, 1)
    all_vectors = [jnp.where(row == step, coarse[k], vectors_in[k]) for k in R3]
    largest = jnp.maximum(jnp.maximum(jnp.abs(all_vectors[0]), jnp.abs(all_vectors[1])), jnp.abs(all_vectors[2]))
    largest = jnp.broadcast_to(jnp.max(largest, axis=1, keepdims=True), shape)
    scale, inverse = power_of_two(largest)
    unit = [all_vectors[k] * inverse for k in R3]
    out = jnp.zeros(shape, f32)
    for lag in range(KC + 1):
        other = [pltpu.roll(u, 8 - lag, 0) if lag else u for u in unit]
        total = dd_total([two_product(unit[k], other[k]) for k in R3])
        sums = [jnp.broadcast_to(jnp.sum(part, axis=1, keepdims=True), shape) for part in limbs(total)]
        total = two_sum(sums[0], sums[1])
        total = quick_sum(total[0], total[1] + sums[2])
        scale_j, inverse_j = (pltpu.roll(s, 8 - lag, 0) if lag else s for s in (scale, inverse))
        pair = row + LAG_START[lag]
        here = row < LAG_COUNT[lag]
        for slot, value in enumerate((*total, scale, scale, scale_j, scale_j, inverse, inverse_j)):
            out = jnp.where(here & (lane == pair + 16 * slot), value, out)
    line = jnp.sum(out, axis=0, keepdims=True)
    payload[...] = jnp.broadcast_to(line, payload.shape)


def combine(gathered):
    n = gathered.shape[0]
    inverse = jnp.min(gathered[...], axis=0, keepdims=True)
    inverse_i = pltpu.roll(jnp.broadcast_to(inverse, (8, LANES)), 32, 1)
    inverse_j = pltpu.roll(jnp.broadcast_to(inverse, (8, LANES)), 16, 1)
    lane = iota((8, LANES), 1)
    inv_i = jnp.where(lane < 16, inverse_i, pltpu.roll(inverse_i, 16, 1))
    inv_j = jnp.where(lane < 16, inverse_j, pltpu.roll(inverse_j, 16, 1))
    terms = []
    for start in range(0, n, 8):
        block = gathered[start : start + 8, :]
        weight = (pltpu.roll(block, LANES - 32, 1) * inv_i) * (pltpu.roll(block, LANES - 64, 1) * inv_j)
        terms.append((jnp.where(lane < 32, block * weight, 0.0), jnp.zeros((8, LANES), f32)))
    total = dd_total(terms)
    for by in (4, 2, 1):
        total = dd_add(total, tuple(pltpu.roll(t, by, 0) for t in total))
    total = dd_add(total, (pltpu.roll(total[0], LANES - 16, 1), jnp.zeros((8, LANES), f32)))

    def spread(value, at):
        return jnp.broadcast_to(value[:, at : at + 1], (8, LANES))

    gram = {}
    for p, (i, j) in enumerate(PAIRS):
        gram[i, j] = gram[j, i] = (spread(total[0], p), spread(total[1], p))
    at_i = {i: p for p, (i, j) in enumerate(PAIRS) if j == i}
    unscale = [spread(inverse_i, at_i[i]) for i in range(KC)] + [spread(inverse_j, PAIRS.index((0, KC)))]
    scale0 = power_of_two(1.25 / unscale[0])[0]
    growth = [power_of_two(1.25 * unscale[j] / unscale[j + 1])[0] for j in range(KC)]
    zero = jnp.zeros((8, LANES), f32)
    one = jnp.ones((8, LANES), f32)
    residual = [(one, zero)]
    direction = [(one, zero)]
    answer = []
    rr = gram[0, 0]
    start = rr[0]
    inverse_rr = 1.0 / rr[0]
    for it in range(KC):
        image = [None] + [(growth[j] * d[0], growth[j] * d[1]) for j, d in enumerate(direction)]
        last = it + 1 == KC
        rows = [
            dd_total([dd_mul(gram[i, j], image[j]) for j in range(1, it + 2)]) for i in range(it + 1 if last else it + 2)
        ]
        curvature = dd_total([dd_mul(direction[i], rows[i]) for i in range(it + 1)])
        live = rr[0] > 1e-12 * start
        curvature = tuple(jnp.where(live, c, o) for c, o in zip(curvature, (one, zero)))
        alpha = dd_div(rr, curvature, 1.0 / curvature[0])
        alpha = tuple(jnp.where(live, a, 0.0) for a in alpha)
        steps = [dd_mul(alpha, d) for d in direction]
        answer = [dd_add(a, s) for a, s in zip(answer, steps)] + steps[len(answer) :]
        if last:
            break
        square = dd_total([dd_mul(image[i], rows[i]) for i in range(1, it + 2)])
        new = dd_add(dd_mul(quick_sum(*dd_mul(alpha, alpha)), square), dd_neg(rr))
        new = tuple(jnp.where(live, n, 0.0) for n in new)
        moved = [None] + [dd_neg(dd_mul(alpha, image[j])) for j in range(1, it + 2)]
        residual = [residual[0]] + [
            dd_add(residual[j], moved[j]) if j < len(residual) else quick_sum(*moved[j]) for j in range(1, it + 2)
        ]
        beta = dd_div(new, rr, inverse_rr)
        direction = [dd_add(residual[j], dd_mul(beta, direction[j])) for j in range(it + 1)] + residual[it + 1 :]
        rr = new
        inverse_rr = 1.0 / jnp.where(rr[0] > 0.0, rr[0], 1.0)
    return [a[0] * (scale0 * unscale[j]) for j, a in enumerate(answer)]


def finish_kernel(gathered, vectors, source, inverse, diagonal, coupling, *refs):
    parts, refs = refs[: KC + 1], refs[KC + 1 :]
    received, (correction, new_field) = refs[: 4 * (KC + 1)], refs[4 * (KC + 1) :]
    weights = combine(gathered)
    for k in R3:
        total = None
        for j in range(KC):
            part = weights[j][0:1] * vectors[k, j : j + 1, :]
            total = part if total is None else total + part
        correction[k] = total
    own = load_field(parts[0])
    nx = len(own[0])
    around = read_halos(received[:4], nx, 1)
    for j in range(KC):
        weight = weights[j]
        own = [[own[c][x] + weight * parts[j + 1][c, x] for x in range(nx)] for c in R3]
        part = read_halos(received[4 * (j + 1) : 4 * (j + 2)], nx, 1 if j + 1 < KC else 0)
        around = (
            [a + weight * b for a, b in zip(around[0], part[0])],
            [a + weight * b for a, b in zip(around[1], part[1])],
            around[2] + weight[0:1] * part[2],
            around[3] + weight[0:1] * part[3],
        )
    image = apply_operator(own, halos(around, nx), diagonal, coupling)
    store_field(new_field, relaxed(own, defect_of(source, image), inverse))


def call(kernel, out_shapes, inputs, scratch=(), dtype=f32):
    return pl.pallas_call(
        kernel,
        out_shape=[jax.ShapeDtypeStruct(s, dtype) for s in out_shapes],
        in_specs=[pl.BlockSpec(memory_space=VMEM)] * len(inputs),
        out_specs=[pl.BlockSpec(memory_space=VMEM)] * len(out_shapes),
        scratch_shapes=list(scratch),
        compiler_params=pltpu.CompilerParams(vmem_limit_bytes=16 * 2**20),
    )(*inputs)


def local(source, initial_guess, coupling, diagonal_block, prolongator, aggregate):
    _, nx, ny, nz = source.shape
    devices = lax.axis_size("sx") * lax.axis_size("sy")
    shape = source.shape
    vector_shape = (3, 8, LANES)
    rows = [pltpu.VMEM((nx * ny * 24, nz), f32)]

    def send_shapes(fields):
        faces, lines = (3 * fields, ny, nz), (3 * fields * ny, nz)
        return [lines, faces, lines, faces]

    received = exchange(call(faces_kernel, send_shapes(1), (initial_guess, coupling)))
    (inverse,) = call(inverse_kernel, [diagonal_block.shape], (diagonal_block,))
    (members,) = call(members_kernel, [(nx * ny * nz, NA)], (aggregate,), dtype=bf16)
    inverse, members, *received = lax.optimization_barrier((inverse, members, *received))
    field = initial_guess
    for _ in range(NU):
        field, *sends = call(
            sweep_kernel, [shape] + send_shapes(1), (field, source, inverse, diagonal_block, coupling, *received)
        )
        received = exchange(sends)
    vectors, fine, further, *sends = call(
        residual_kernel,
        [vector_shape, shape, shape] + send_shapes(2),
        (field, source, inverse, diagonal_block, coupling, prolongator, aggregate, members, *received),
        rows,
    )
    parts, around = [further], [exchange(sends)]
    for step in range(1, KC):
        vectors, fine, further, *sends = call(
            functools.partial(krylov_kernel, step),
            [vector_shape, shape, shape] + send_shapes(2),
            (fine, vectors, inverse, diagonal_block, coupling, prolongator, aggregate, members, *around[-1]),
            rows,
        )
        parts.append(further)
        around.append(exchange(sends))
    payload, further, *sends = call(
        functools.partial(gram_kernel, KC),
        [(devices, LANES), shape] + send_shapes(1),
        (fine, vectors, inverse, diagonal_block, coupling, prolongator, aggregate, members, *around[-1]),
        rows,
    )
    parts.append(further)
    around.append(exchange(sends))
    gathered = lax.all_to_all(payload.reshape(devices, 1, LANES), ("sx", "sy"), 0, 0).reshape(devices, LANES)
    correction, field = call(
        finish_kernel,
        [(3, 1, LANES), shape],
        (gathered, vectors, source, inverse, diagonal_block, coupling, *parts) + tuple(h for halo in around for h in halo),
    )
    return field, correction.reshape(3, 1, 1, NA)


def solution(mesh):
    in_specs = (
        P(None, "sx", "sy", None),
        P(None, "sx", "sy", None),
        P(None, None, None, "sx", "sy", None),
        P(None, None, "sx", "sy", None),
        P(None, None, "sx", "sy", None),
        P("sx", "sy", None),
    )
    out_specs = (P(None, "sx", "sy", None), P(None, "sx", "sy", None))
    return jax.shard_map(local, mesh=mesh, in_specs=in_specs, out_specs=out_specs, check_vma=False)
```

```python
import functools

import jax
import jax.numpy as jnp
from jax import lax
from jax.experimental import pallas as pl
from jax.experimental.pallas import tpu as pltpu
from jax.sharding import PartitionSpec as P

NU = 2
KC = 4
NA = 128
LANES = 128

damping = 0.8
R3 = range(3)
VMEM = pltpu.VMEM
f32 = jnp.float32
bf16 = jnp.bfloat16

PAIRS = [(i, i + lag) for lag in range(KC + 1) for i in range(KC) if i + lag <= KC]
LAG_START = [min(p for p, (i, j) in enumerate(PAIRS) if j - i == lag) for lag in range(KC + 1)]
LAG_COUNT = [sum(1 for i, j in PAIRS if j - i == lag) for lag in range(KC + 1)]


def pair_exchange(x, axis, odd):
    n = lax.axis_size(axis)
    if odd:
        pairs = [(k, (k + 1) % n) for k in range(1, n, 2)] + [((k + 1) % n, k) for k in range(1, n, 2)]
    else:
        pairs = [(k, k ^ 1) for k in range(n)]
    return lax.ppermute(x, axis, pairs)


def exchange(sends):
    yb, xb, ya, xa = sends
    return (
        pair_exchange(yb, "sy", True),
        pair_exchange(xb, "sx", True),
        pair_exchange(ya, "sy", False),
        pair_exchange(xa, "sx", False),
    )


def iota(shape, dim):
    return lax.broadcasted_iota(jnp.int32, shape, dim)


def sides(axis):
    index = lax.axis_index(axis)
    return index % 2 == 0, index == 0, index == lax.axis_size(axis) - 1


def load_field(ref):
    return [[ref[c, x] for x in range(ref.shape[1])] for c in R3]


def store_field(ref, field):
    for c in R3:
        for x in range(ref.shape[1]):
            ref[c, x] = field[c][x]


def times(block, vector):
    return [block(i, 0) * vector[0] + block(i, 1) * vector[1] + block(i, 2) * vector[2] for i in R3]


def transposed_times(block, vector):
    return [block(0, i) * vector[0] + block(1, i) * vector[1] + block(2, i) * vector[2] for i in R3]


def send_faces(fields, coupling, sends):
    yb, xb, ya, xa = sends
    nx = len(fields[0][0])
    ny = fields[0][0][0].shape[0]
    even_x, _, _ = sides("sx")
    even_y, _, _ = sides("sy")
    for number, field in enumerate(fields):
        for x in range(nx):
            top = transposed_times(
                lambda i, j: coupling[1, i, j, x, ny - 1 : ny], [field[j][x][ny - 1 : ny] for j in R3]
            )
            for i in R3:
                bottom = field[i][x][0:1]
                row = (3 * number + i) * nx + x
                ya[row : row + 1] = jnp.where(even_y, top[i], bottom)
                yb[row : row + 1] = jnp.where(even_y, bottom, top[i])
        top = transposed_times(lambda i, j: coupling[0, i, j, nx - 1], [field[j][nx - 1] for j in R3])
        for i in R3:
            bottom = field[i][0]
            xa[3 * number + i] = jnp.where(even_x, top[i], bottom)
            xb[3 * number + i] = jnp.where(even_x, bottom, top[i])


def halos(received, nx):
    xa, xb, ya, yb = received
    even_x, first_x, last_x = sides("sx")
    even_y, first_y, last_y = sides("sy")
    up_x = [jnp.where(last_x, 0.0, jnp.where(even_x, xa[i], xb[i])) for i in R3]
    low_x = [jnp.where(first_x, 0.0, jnp.where(even_x, xb[i], xa[i])) for i in R3]
    up_y = jnp.where(last_y, 0.0, jnp.where(even_y, ya, yb))
    low_y = jnp.where(first_y, 0.0, jnp.where(even_y, yb, ya))
    up_y = [[up_y[i * nx + x : i * nx + x + 1] for x in range(nx)] for i in R3]
    low_y = [[low_y[i * nx + x : i * nx + x + 1] for x in range(nx)] for i in R3]
    return up_x, low_x, up_y, low_y


def read_halos(refs, nx, number=0):
    yb, xb, ya, xa = refs
    at = 3 * number
    rows = slice(at * nx, (at + 3) * nx)
    return [xa[at + i] for i in R3], [xb[at + i] for i in R3], ya[rows], yb[rows]


def apply_operator(field, around, diagonal, coupling):
    up_x, low_x, up_y, low_y = around
    nx = len(field[0])
    ny, nz = field[0][0].shape
    row = iota((ny, nz), 0)
    lane = iota((ny, nz), 1)
    result = [[None] * nx for _ in R3]
    for x in range(nx):
        own = [field[j][x] for j in R3]
        total = times(lambda i, j: diagonal[i, j, x], own)
        upper = [field[j][x + 1] if x + 1 < nx else up_x[j] for j in R3]
        part = times(lambda i, j: coupling[0, i, j, x], upper)
        total = [total[i] + part[i] for i in R3]
        if x:
            part = transposed_times(lambda i, j: coupling[0, i, j, x - 1], [field[j][x - 1] for j in R3])
        else:
            part = low_x
        total = [total[i] + part[i] for i in R3]
        upper = [jnp.where(row == ny - 1, up_y[j][x], pltpu.roll(own[j], ny - 1, 0)) for j in R3]
        part = times(lambda i, j: coupling[1, i, j, x], upper)
        total = [total[i] + part[i] for i in R3]
        part = transposed_times(lambda i, j: coupling[1, i, j, x], own)
        total = [total[i] + jnp.where(row == 0, low_y[i][x], pltpu.roll(part[i], 1, 0)) for i in R3]
        upper = [jnp.where(lane == nz - 1, 0.0, pltpu.roll(own[j], nz - 1, 1)) for j in R3]
        part = times(lambda i, j: coupling[2, i, j, x], upper)
        total = [total[i] + part[i] for i in R3]
        part = transposed_times(lambda i, j: coupling[2, i, j, x], own)
        total = [total[i] + jnp.where(lane == 0, 0.0, pltpu.roll(part[i], 1, 1)) for i in R3]
        for i in R3:
            result[i][x] = total[i]
    return result


def inverse_of(diagonal, x):
    m = [[diagonal[i, j, x] for j in R3] for i in R3]
    adjugate = [
        [
            m[(j + 1) % 3][(i + 1) % 3] * m[(j + 2) % 3][(i + 2) % 3]
            - m[(j + 1) % 3][(i + 2) % 3] * m[(j + 2) % 3][(i + 1) % 3]
            for j in R3
        ]
        for i in R3
    ]
    determinant = m[0][0] * adjugate[0][0] + m[0][1] * adjugate[1][0] + m[0][2] * adjugate[2][0]
    return [[adjugate[i][j] / determinant for j in R3] for i in R3]


def relaxed(field, defect, inverse):
    result = [[None] * len(field[0]) for _ in R3]
    for x in range(len(field[0])):
        change = times(lambda i, j: inverse[i, j, x], [defect[i][x] for i in R3])
        for i in R3:
            result[i][x] = field[i][x] + damping * change[i]
    return result


def defect_of(source, image):
    return [[source[i, x] - image[i][x] for x in range(len(image[0]))] for i in R3]


def negated(image):
    return [[-value for value in row] for row in image]


def restrict(field, prolongator, members, rows):
    nx = len(field[0])
    ny, nz = field[0][0].shape
    for x in range(nx):
        values = transposed_times(lambda i, j: prolongator[i, j, x], [field[j][x] for j in R3])
        for k in R3:
            high = values[k].astype(bf16).astype(f32)
            rest = values[k] - high
            middle = rest.astype(bf16).astype(f32)
            low = rest - middle
            for part, value in enumerate((high, middle, low)):
                rows[pl.ds(x * ny * 24 + 3 * part + k, ny, stride=24), :] = value
    left = [rows[block * 24 : block * 24 + 16, :].astype(bf16) for block in range(nx * ny)]
    total = lax.dot_general(
        jnp.concatenate(left, axis=1), members[...], (((1,), (0,)), ((), ())), preferred_element_type=f32
    )
    return [total[k : k + 1] + (total[3 + k : 4 + k] + total[6 + k : 7 + k]) for k in R3]


def prolong(coarse, prolongator, aggregate):
    nx, ny, nz = aggregate.shape
    tables = [jnp.broadcast_to(coarse[k], (ny, nz)) for k in R3]
    result = [[None] * nx for _ in R3]
    for x in range(nx):
        ids = aggregate[x]
        picked = [jnp.take_along_axis(tables[k], ids, axis=1, mode="promise_in_bounds") for k in R3]
        value = times(lambda i, j: prolongator[i, j, x], picked)
        for i in R3:
            result[i][x] = value[i]
    return result


def two_sum(a, b):
    s = a + b
    t = s - a
    return s, (a - (s - t)) + (b - t)


def quick_sum(a, b):
    s = a + b
    return s, b - (s - a)


def halves(a):
    c = 4097.0 * a
    high = c - (c - a)
    return high, a - high


def two_product(a, b):
    p = a * b
    ah, al = halves(a)
    bh, bl = halves(b)
    return p, ((ah * bh - p) + ah * bl + al * bh) + al * bl


def dd_add(x, y):
    s, e = two_sum(x[0], y[0])
    return quick_sum(s, e + (x[1] + y[1]))


def dd_neg(x):
    return -x[0], -x[1]


def dd_mul(x, y):
    p, e = two_product(x[0], y[0])
    return p, e + (x[0] * y[1] + x[1] * y[0])


def dd_div(x, y, inverse):
    first = x[0] * inverse
    p, e = two_product(first, y[0])
    rest = ((x[0] - p) - e) + (x[1] - first * y[1])
    return quick_sum(first, rest * inverse)


def plain_total(terms):
    while len(terms) > 1:
        terms = [terms[k] + terms[k + 1] if k + 1 < len(terms) else terms[k] for k in range(0, len(terms), 2)]
    return terms[0]


def dd_total(terms):
    highs, lows = [t[0] for t in terms], [plain_total([t[1] for t in terms])]
    while len(highs) > 1:
        pairs = [two_sum(highs[k], highs[k + 1]) for k in range(0, len(highs) - 1, 2)]
        lows += [e for _, e in pairs]
        highs = [s for s, _ in pairs] + highs[2 * len(pairs) :]
    return quick_sum(highs[0], plain_total(lows))


def limbs(total):
    first = (total[0] + 1536.0) - 1536.0
    rest = total[0] - first
    second = (rest + 1.5 * 2.0**-7) - 1.5 * 2.0**-7
    return first, second, (rest - second) + total[1]


def power_of_two(x):
    scale = jnp.full_like(x, 2.0**-126)
    inverse = jnp.full_like(x, 2.0**126)
    for step in (64, 64, 64, 32, 16, 8, 4, 2, 1):
        larger = scale * 2.0**step
        take = (x >= larger) & (larger <= 2.0**126)
        scale = jnp.where(take, larger, scale)
        inverse = jnp.where(take, inverse * 2.0**-step, inverse)
    return scale, inverse


def members_kernel(aggregate, members):
    nx, ny, nz = aggregate.shape
    which = iota((nz, NA), 1)
    for x in range(nx):
        ids = jnp.transpose(aggregate[x].astype(f32)).astype(jnp.int32)
        for y in range(ny):
            own = jnp.broadcast_to(ids[:, y : y + 1], (nz, NA))
            at = (x * ny + y) * nz
            members[at : at + nz, :] = jnp.where(own == which, 1.0, 0.0).astype(bf16)


def inverse_kernel(diagonal, inverse):
    for x in range(diagonal.shape[2]):
        block = inverse_of(diagonal, x)
        for i in R3:
            for j in R3:
                inverse[i, j, x] = block[i][j]


def faces_kernel(field, coupling, *sends):
    send_faces([load_field(field)], coupling, sends)


def sweep_kernel(field, source, inverse, diagonal, coupling, *refs):
    received, new_field, sends = refs[:4], refs[4], refs[5:]
    own = load_field(field)
    nx = len(own[0])
    image = apply_operator(own, halos(read_halos(received, nx), nx), diagonal, coupling)
    new = relaxed(own, defect_of(source, image), inverse)
    store_field(new_field, new)
    send_faces([new], coupling, sends)


def residual_kernel(field, source, inverse, diagonal, coupling, prolongator, aggregate, members, *refs):
    received, (vectors, fine, further), sends, rows = refs[:4], refs[4:7], refs[7:11], refs[11]
    own = load_field(field)
    nx = len(own[0])
    image = apply_operator(own, halos(read_halos(received, nx), nx), diagonal, coupling)
    defect = defect_of(source, image)
    coarse = restrict(defect, prolongator, members, rows)
    row = iota((8, LANES), 0)
    for k in R3:
        vectors[k] = jnp.where(row == 0, coarse[k], 0.0)
    new = prolong(coarse, prolongator, aggregate)
    store_field(fine, new)
    swept = relaxed(own, defect, inverse)
    store_field(further, swept)
    send_faces([new, swept], coupling, sends)


def krylov_kernel(step, fine_in, vectors_in, inverse, diagonal, coupling, prolongator, aggregate, members, *refs):
    received, (vectors, fine, further), sends, rows = refs[:4], refs[4:7], refs[7:11], refs[11]
    own = load_field(fine_in)
    nx = len(own[0])
    image = apply_operator(own, halos(read_halos(received, nx), nx), diagonal, coupling)
    coarse = restrict(image, prolongator, members, rows)
    row = iota((8, LANES), 0)
    for k in R3:
        vectors[k] = jnp.where(row == step, coarse[k], vectors_in[k])
    new = prolong(coarse, prolongator, aggregate)
    store_field(fine, new)
    swept = relaxed(own, negated(image), inverse)
    store_field(further, swept)
    send_faces([new, swept], coupling, sends)


def gram_kernel(step, fine_in, vectors_in, inverse, diagonal, coupling, prolongator, aggregate, members, *refs):
    received, payload, further, sends, rows = refs[:4], refs[4], refs[5], refs[6:10], refs[10]
    own = load_field(fine_in)
    nx = len(own[0])
    image = apply_operator(own, halos(read_halos(received, nx), nx), diagonal, coupling)
    swept = relaxed(own, negated(image), inverse)
    store_field(further, swept)
    send_faces([swept], coupling, sends)
    coarse = restrict(image, prolongator, members, rows)
    shape = (8, LANES)
    row, lane = iota(shape, 0), iota(shape, 1)
    all_vectors = [jnp.where(row == step, coarse[k], vectors_in[k]) for k in R3]
    largest = jnp.maximum(jnp.maximum(jnp.abs(all_vectors[0]), jnp.abs(all_vectors[1])), jnp.abs(all_vectors[2]))
    largest = jnp.broadcast_to(jnp.max(largest, axis=1, keepdims=True), shape)
    scale, inverse = power_of_two(largest)
    unit = [all_vectors[k] * inverse for k in R3]
    out = jnp.zeros(shape, f32)
    for lag in range(KC + 1):
        other = [pltpu.roll(u, 8 - lag, 0) if lag else u for u in unit]
        total = dd_total([two_product(unit[k], other[k]) for k in R3])
        sums = [jnp.broadcast_to(jnp.sum(part, axis=1, keepdims=True), shape) for part in limbs(total)]
        total = two_sum(sums[0], sums[1])
        total = quick_sum(total[0], total[1] + sums[2])
        scale_j, inverse_j = (pltpu.roll(s, 8 - lag, 0) if lag else s for s in (scale, inverse))
        pair = row + LAG_START[lag]
        here = row < LAG_COUNT[lag]
        for slot, value in enumerate((*total, scale, scale, scale_j, scale_j, inverse, inverse_j)):
            out = jnp.where(here & (lane == pair + 16 * slot), value, out)
    line = jnp.sum(out, axis=0, keepdims=True)
    payload[...] = jnp.broadcast_to(line, payload.shape)


def combine(gathered):
    n = gathered.shape[0]
    inverse = jnp.min(gathered[...], axis=0, keepdims=True)
    inverse_i = pltpu.roll(jnp.broadcast_to(inverse, (8, LANES)), 32, 1)
    inverse_j = pltpu.roll(jnp.broadcast_to(inverse, (8, LANES)), 16, 1)
    lane = iota((8, LANES), 1)
    inv_i = jnp.where(lane < 16, inverse_i, pltpu.roll(inverse_i, 16, 1))
    inv_j = jnp.where(lane < 16, inverse_j, pltpu.roll(inverse_j, 16, 1))
    terms = []
    for start in range(0, n, 8):
        block = gathered[start : start + 8, :]
        weight = (pltpu.roll(block, LANES - 32, 1) * inv_i) * (pltpu.roll(block, LANES - 64, 1) * inv_j)
        terms.append((jnp.where(lane < 32, block * weight, 0.0), jnp.zeros((8, LANES), f32)))
    total = dd_total(terms)
    for by in (4, 2, 1):
        total = dd_add(total, tuple(pltpu.roll(t, by, 0) for t in total))
    total = dd_add(total, (pltpu.roll(total[0], LANES - 16, 1), jnp.zeros((8, LANES), f32)))

    def spread(value, at):
        return jnp.broadcast_to(value[:, at : at + 1], (8, LANES))

    gram = {}
    for p, (i, j) in enumerate(PAIRS):
        gram[i, j] = gram[j, i] = (spread(total[0], p), spread(total[1], p))
    at_i = {i: p for p, (i, j) in enumerate(PAIRS) if j == i}
    unscale = [spread(inverse_i, at_i[i]) for i in range(KC)] + [spread(inverse_j, PAIRS.index((0, KC)))]
    scale0 = power_of_two(1.25 / unscale[0])[0]
    growth = [power_of_two(1.25 * unscale[j] / unscale[j + 1])[0] for j in range(KC)]
    zero = jnp.zeros((8, LANES), f32)
    one = jnp.ones((8, LANES), f32)
    residual = [(one, zero)]
    direction = [(one, zero)]
    answer = []
    rr = gram[0, 0]
    start = rr[0]
    inverse_rr = 1.0 / rr[0]
    for it in range(KC):
        image = [None] + [(growth[j] * d[0], growth[j] * d[1]) for j, d in enumerate(direction)]
        last = it + 1 == KC
        rows = [
            dd_total([dd_mul(gram[i, j], image[j]) for j in range(1, it + 2)]) for i in range(it + 1 if last else it + 2)
        ]
        curvature = dd_total([dd_mul(direction[i], rows[i]) for i in range(it + 1)])
        live = rr[0] > 1e-12 * start
        curvature = tuple(jnp.where(live, c, o) for c, o in zip(curvature, (one, zero)))
        alpha = dd_div(rr, curvature, 1.0 / curvature[0])
        alpha = tuple(jnp.where(live, a, 0.0) for a in alpha)
        steps = [dd_mul(alpha, d) for d in direction]
        answer = [dd_add(a, s) for a, s in zip(answer, steps)] + steps[len(answer) :]
        if last:
            break
        square = dd_total([dd_mul(image[i], rows[i]) for i in range(1, it + 2)])
        new = dd_add(dd_mul(quick_sum(*dd_mul(alpha, alpha)), square), dd_neg(rr))
        new = tuple(jnp.where(live, n, 0.0) for n in new)
        moved = [None] + [dd_neg(dd_mul(alpha, image[j])) for j in range(1, it + 2)]
        residual = [residual[0]] + [
            dd_add(residual[j], moved[j]) if j < len(residual) else quick_sum(*moved[j]) for j in range(1, it + 2)
        ]
        beta = dd_div(new, rr, inverse_rr)
        direction = [dd_add(residual[j], dd_mul(beta, direction[j])) for j in range(it + 1)] + residual[it + 1 :]
        rr = new
        inverse_rr = 1.0 / jnp.where(rr[0] > 0.0, rr[0], 1.0)
    return [a[0] * (scale0 * unscale[j]) for j, a in enumerate(answer)]


def finish_kernel(gathered, vectors, source, inverse, diagonal, coupling, *refs):
    parts, refs = refs[: KC + 1], refs[KC + 1 :]
    received, (correction, new_field) = refs[: 4 * (KC + 1)], refs[4 * (KC + 1) :]
    weights = combine(gathered)
    for k in R3:
        total = None
        for j in range(KC):
            part = weights[j][0:1] * vectors[k, j : j + 1, :]
            total = part if total is None else total + part
        correction[k] = total
    own = load_field(parts[0])
    nx = len(own[0])
    around = read_halos(received[:4], nx, 1)
    for j in range(KC):
        weight = weights[j]
        own = [[own[c][x] + weight * parts[j + 1][c, x] for x in range(nx)] for c in R3]
        part = read_halos(received[4 * (j + 1) : 4 * (j + 2)], nx, 1 if j + 1 < KC else 0)
        around = (
            [a + weight * b for a, b in zip(around[0], part[0])],
            [a + weight * b for a, b in zip(around[1], part[1])],
            around[2] + weight[0:1] * part[2],
            around[3] + weight[0:1] * part[3],
        )
    image = apply_operator(own, halos(around, nx), diagonal, coupling)
    store_field(new_field, relaxed(own, defect_of(source, image), inverse))


def call(kernel, out_shapes, inputs, scratch=(), dtype=f32):
    return pl.pallas_call(
        kernel,
        out_shape=[jax.ShapeDtypeStruct(s, dtype) for s in out_shapes],
        in_specs=[pl.BlockSpec(memory_space=VMEM)] * len(inputs),
        out_specs=[pl.BlockSpec(memory_space=VMEM)] * len(out_shapes),
        scratch_shapes=list(scratch),
        compiler_params=pltpu.CompilerParams(vmem_limit_bytes=16 * 2**20),
    )(*inputs)


def local(source, initial_guess, coupling, diagonal_block, prolongator, aggregate):
    _, nx, ny, nz = source.shape
    devices = lax.axis_size("sx") * lax.axis_size("sy")
    shape = source.shape
    vector_shape = (3, 8, LANES)
    rows = [pltpu.VMEM((nx * ny * 24 + 24, nz), f32)]

    def send_shapes(fields):
        faces, lines = (3 * fields, ny, nz), (3 * fields * ny, nz)
        return [lines, faces, lines, faces]

    received = exchange(call(faces_kernel, send_shapes(1), (initial_guess, coupling)))
    (inverse,) = call(inverse_kernel, [diagonal_block.shape], (diagonal_block,))
    (members,) = call(members_kernel, [(nx * ny * nz, NA)], (aggregate,), dtype=bf16)
    inverse, members, *received = lax.optimization_barrier((inverse, members, *received))
    field = initial_guess
    for _ in range(NU):
        field, *sends = call(
            sweep_kernel, [shape] + send_shapes(1), (field, source, inverse, diagonal_block, coupling, *received)
        )
        received = exchange(sends)
    vectors, fine, further, *sends = call(
        residual_kernel,
        [vector_shape, shape, shape] + send_shapes(2),
        (field, source, inverse, diagonal_block, coupling, prolongator, aggregate, members, *received),
        rows,
    )
    parts, around = [further], [exchange(sends)]
    for step in range(1, KC):
        vectors, fine, further, *sends = call(
            functools.partial(krylov_kernel, step),
            [vector_shape, shape, shape] + send_shapes(2),
            (fine, vectors, inverse, diagonal_block, coupling, prolongator, aggregate, members, *around[-1]),
            rows,
        )
        parts.append(further)
        around.append(exchange(sends))
    payload, further, *sends = call(
        functools.partial(gram_kernel, KC),
        [(devices, LANES), shape] + send_shapes(1),
        (fine, vectors, inverse, diagonal_block, coupling, prolongator, aggregate, members, *around[-1]),
        rows,
    )
    parts.append(further)
    around.append(exchange(sends))
    gathered = lax.all_to_all(payload.reshape(devices, 1, LANES), ("sx", "sy"), 0, 0).reshape(devices, LANES)
    correction, field = call(
        finish_kernel,
        [(3, 1, LANES), shape],
        (gathered, vectors, source, inverse, diagonal_block, coupling, *parts) + tuple(h for halo in around for h in halo),
    )
    return field, correction.reshape(3, 1, 1, NA)


def solution(mesh):
    in_specs = (
        P(None, "sx", "sy", None),
        P(None, "sx", "sy", None),
        P(None, None, None, "sx", "sy", None),
        P(None, None, "sx", "sy", None),
        P(None, None, "sx", "sy", None),
        P("sx", "sy", None),
    )
    out_specs = (P(None, "sx", "sy", None), P(None, "sx", "sy", None))
    return jax.shard_map(local, mesh=mesh, in_specs=in_specs, out_specs=out_specs, check_vma=False)
```
